512 devices in a mesh: blk: 64 (over x, y_lo, z), rep: 8 (over y_hi, core).
Axes of the slice: x: 4, y: 8 (y_hi: 4, y_lo: 2; y = y_hi * 2 + y_lo), z: 8, core: 2. Of those that a mesh axis runs over, the one named last changes fastest.
Arguments:
- position: float32 [3, 524288], P(None, 'blk'), may hold values from -6 to 6
- velocity: float32 [3, 524288], P(None, 'blk'), may hold values from -6 to 6
- accel: float32 [3, 524288], P(None, 'blk'), may hold values from -6 to 6
- jerk: float32 [3, 524288], P(None, 'blk'), may hold values from -12 to 12
- mass: float32 [524288], P('blk'), may hold values from 0.1 to 10
- elapsed: float32 [524288], P('blk'), may hold values from 0.02 to 0.25
- active_index: int32 [16384], P('blk'), may hold values from -1 to 524287, as said below
Outputs:
- force: float32 [3, 16384], P(None, 'blk')
- new_jerk: float32 [3, 16384], P(None, 'blk')
The draws below stay inside these ranges and needn't reach their ends.
Inputs may be any that keep to these rules, and one draw needn't show every extreme that they name: `active_index`: each team t has 256 slots; they hold the indices of active stars of that team (t * 8192 to (t + 1) * 8192 - 1) in increasing order, then -1 in the remaining slots. Every team has at least one active star, and in every draw some team has all 256 slots filled; the counts differ strongly from team to team.
All inputs are finite; a program needn't handle non-finite values.
Results may differ from the reference program's by a relative error of at most 0.0003.
Values sent between devices are 32-bit elements; how exact they have to be, the bound alone decides.
A program may use at most 64 MiB of HBM per device.

```python
import math
import jax
import jax.numpy as jnp
from jax import lax

S_DEV = 8192
CAP = 256
STARS = 524288
SLOTS = 16384


def draw_active_index(key, part):
    teams = SLOTS // CAP
    team_keys = jax.random.split(jax.random.fold_in(key, 11), teams)
    first_key, second_key = jax.random.split(jax.random.fold_in(key, 12), 2)
    tries = jax.random.randint(first_key, (3, teams), 1, CAP + 1)
    counts = jnp.min(tries, axis=0)
    busiest = jax.random.randint(second_key, (), 0, teams)
    counts = jnp.where(jnp.arange(teams) == busiest, CAP, counts)

    def one_team(team_key, count, team):
        order = jax.random.permutation(team_key, S_DEV)[:CAP]
        slot_order = jnp.arange(CAP)
        chosen = jnp.sort(jnp.where(slot_order < count, order, S_DEV))
        return jnp.where(slot_order < count, chosen + team * S_DEV, -1)
    drawn = jax.vmap(one_team)(team_keys, counts, jnp.arange(teams))
    return drawn.reshape(SLOTS).astype(jnp.int32)


def steps_of(own_key, extent, cuts, least, largest):
    def one(dim, blocks):
        steps = jax.random.uniform(jax.random.fold_in(jax.random.fold_in(own_key, 6), dim), (blocks,), jnp.float32, least / len(cuts), largest / len(cuts))
        return jnp.repeat(jnp.exp(steps), extent[dim] // blocks).reshape((-1,) + (1,) * (len(extent) - dim - 1))

    factor_of = one(*cuts[0])
    for cut in cuts[1:]:
        factor_of = factor_of * one(*cut)
    return factor_of


def scatter_about(stream_key, shape, scale, most, cuts=(), held_as=jnp.bfloat16):
    level = steps_of(stream_key, shape, cuts, -0.22, 0.18) if cuts else 1.0
    values = jax.random.normal(stream_key, shape, jnp.float32) * scale * level
    return jnp.minimum(jnp.maximum(values, -most), most).astype(held_as)


def setup_inputs(seed: int = 0) -> dict:
    streams_of = jax.random.split(jax.random.key(seed), 8)
    position = scatter_about(streams_of[0], (3, STARS), 1.0, 6.0, ((1, 64),), jnp.float32)
    velocity = scatter_about(streams_of[1], (3, STARS), 1.0, 6.0, ((1, 64),), jnp.float32)
    accel = scatter_about(streams_of[2], (3, STARS), 1.0, 6.0, ((1, 64),), jnp.float32)
    jerk = scatter_about(streams_of[3], (3, STARS), 2.0, 12.0, ((1, 64),), jnp.float32)
    mass = jnp.clip(jnp.exp(math.log(10.0) - 4.6051702 * jax.random.uniform(streams_of[4], (STARS,), jnp.float32) ** steps_of(streams_of[4], (STARS,), ((0, 64),), -0.2, 0.2)), 0.1, 10.0)
    elapsed = jnp.clip(jnp.exp(math.log(0.25) - 2.5257287 * jax.random.uniform(streams_of[5], (STARS,), jnp.float32) ** steps_of(streams_of[5], (STARS,), ((0, 64),), -0.2, 0.2)), 0.02, 0.25)
    active_index = draw_active_index(jax.random.fold_in(streams_of[7], 71), 0)
    return {"position": position, "velocity": velocity, "accel": accel, "jerk": jerk, "mass": mass, "elapsed": elapsed, "active_index": active_index}


SOFTENING = 0.001

def predict(position, velocity, accel, jerk, elapsed):
    step_time = elapsed[None, :]
    moved = position + step_time * (velocity + step_time * (0.5 * accel + step_time / 6.0 * jerk))
    turned = velocity + step_time * (accel + 0.5 * step_time * jerk)
    return (moved, turned)

def pair_sums(targets, sources, weights):
    delta_one = sources[0][None, :] - targets[0][:, None]
    delta_two = sources[1][None, :] - targets[1][:, None]
    delta_three = sources[2][None, :] - targets[2][:, None]
    drift_one = sources[3][None, :] - targets[3][:, None]
    drift_two = sources[4][None, :] - targets[4][:, None]
    drift_three = sources[5][None, :] - targets[5][:, None]
    radius_sq = delta_one * delta_one + delta_two * delta_two + delta_three * delta_three + SOFTENING
    inverse = lax.rsqrt(radius_sq)
    strength = weights[None, :] * inverse * inverse * inverse
    radial = 3.0 * (delta_one * drift_one + delta_two * drift_two + delta_three * drift_three) * (inverse * inverse)
    pull_one = lax.optimization_barrier(jnp.sum(strength * delta_one, axis=1))
    pull_two = lax.optimization_barrier(jnp.sum(strength * delta_two, axis=1))
    pull_three = lax.optimization_barrier(jnp.sum(strength * delta_three, axis=1))
    twist_one = lax.optimization_barrier(jnp.sum(strength * (drift_one - radial * delta_one), axis=1))
    twist_two = lax.optimization_barrier(jnp.sum(strength * (drift_two - radial * delta_two), axis=1))
    twist_three = lax.optimization_barrier(jnp.sum(strength * (drift_three - radial * delta_three), axis=1))
    return jnp.stack([pull_one, pull_two, pull_three, twist_one, twist_two, twist_three], 0)

def reference(position, velocity, accel, jerk, mass, elapsed, active_index):
    moved, turned = predict(position, velocity, accel, jerk, elapsed)
    field = jnp.concatenate([moved, turned], 0)
    rows = math.gcd(CAP, 32)
    piece = math.gcd(STARS, 16384)

    def one_team(indices):
        live_mask = indices >= 0
        count = jnp.sum(live_mask.astype(jnp.int32))
        targets = jnp.take(field, jnp.maximum(indices, 0).astype(jnp.int32), axis=1)

        def add_rows(block_no, running):
            start = block_no * rows
            chosen = lax.dynamic_slice_in_dim(targets, start, rows, 1)

            def add_piece(piece_no, total):
                begin = piece_no * piece
                sources = lax.dynamic_slice_in_dim(field, begin, piece, 1)
                weights = lax.dynamic_slice_in_dim(mass, begin, piece, 0)
                return total + pair_sums(chosen, sources, weights)
            block_sum = lax.fori_loop(0, STARS // piece, add_piece, jnp.zeros((6, rows), jnp.float32))
            return lax.dynamic_update_slice_in_dim(running, block_sum, start, 1)
        sums = lax.fori_loop(0, (count + rows - 1) // rows, add_rows, jnp.zeros((6, CAP), jnp.float32))
        return jnp.where(live_mask[None, :], sums / STARS, 0.0)
    results = lax.map(one_team, active_index.reshape(STARS // S_DEV, CAP))
    joined = jnp.transpose(results, (1, 0, 2)).reshape(6, SLOTS)
    return (joined[0:3], joined[3:6])
```

```python
import functools

import jax
import jax.numpy as jnp
from jax import lax
from jax.experimental import pallas as pl
from jax.experimental.pallas import tpu as pltpu
from jax.sharding import PartitionSpec as P

SOFTENING = 0.001
MESH = pl.DeviceIdType.MESH
F32 = jnp.float32
BF16 = jnp.bfloat16
TEAMS = 64
REPS = 8
CAP = 256
SHARE = CAP // REPS
STARS_DEV = 8192
MAX_ROWS = TEAMS * SHARE
TB = 64
CHUNK = 1024


def iota(shape, dim):
    return lax.broadcasted_iota(jnp.int32, shape, dim)


def phase_of(team, rep):
    return lax.rem(rep + 3 * team, REPS)


def split3(x):
    a = x.astype(BF16)
    rest = x - a.astype(F32)
    b = rest.astype(BF16)
    c = (rest - b.astype(F32)).astype(BF16)
    return a, b, c


def fanned(rows, unit):
    sub = lax.rem(iota((8, 128), 0), 4)
    out = rows
    for k in range(1, 4):
        out = jnp.where(sub == k, pltpu.roll(rows, unit * k % 128, 1), out)
    return out


def signal_peers(barrier, axis, me, size):
    def one(step, carry):
        pl.semaphore_signal(
            barrier, inc=1, device_id={axis: lax.rem(me + step, size)}, device_id_type=MESH
        )
        return carry

    lax.fori_loop(1, size, one, 0)


def predict_kernel(index_ref, pos, vel, acc, jrk, mass, elapsed, own, field):
    team = lax.axis_index("blk")
    rep = lax.axis_index("rep")
    h = elapsed[...]
    v, a, j = vel[...], acc[...], jrk[...]
    field[0:3, :] = pos[...] + h * (v + h * (0.5 * a + h / 6.0 * j))
    field[3:6, :] = v + h * (a + 0.5 * h * j)
    field[6:7, :] = jnp.ones((1, STARS_DEV), F32)
    field[7:8, :] = jnp.zeros((1, STARS_DEV), F32)

    phase = phase_of(team, rep)
    lane = iota((8, 128), 1)
    sub = iota((8, 128), 0)
    picked = jnp.zeros((8, 128), F32)
    for k in range(SHARE):
        index = index_ref[REPS * k + phase]
        local = jnp.clip(index - team * STARS_DEV, 0, STARS_DEV - 1)
        tile = field[:, pl.ds(pl.multiple_of(lax.div(local, 128) * 128, 128), 128)]
        turned = pltpu.roll(tile, lax.rem(k - lax.rem(local, 128) + 128, 128), 1)
        picked = jnp.where((lane == k) & (index >= 0), turned, picked)
    spread = fanned(picked, 32)
    spread = jnp.where(lane // 32 == lax.rem(sub, 4), spread, 0.0)
    own[...] = jnp.concatenate(
        [jnp.sum(spread[0:4], axis=0, keepdims=True), jnp.sum(spread[4:8], axis=0, keepdims=True)], 0
    )
    field[6:7, :] = mass[...]


def share_kernel(own, targets_out, offset_out, recv, send_sem, recv_sem):
    team = lax.axis_index("blk")
    barrier = pltpu.get_barrier_semaphore()
    signal_peers(barrier, "blk", team, TEAMS)
    recv[team] = own[...]
    pl.semaphore_wait(barrier, TEAMS - 1)

    def send(step, carry):
        pltpu.make_async_remote_copy(
            src_ref=own,
            dst_ref=recv.at[team],
            send_sem=send_sem,
            recv_sem=recv_sem,
            device_id={"blk": lax.rem(team + step, TEAMS)},
            device_id_type=MESH,
        ).start()
        return carry

    lax.fori_loop(1, TEAMS, send, 0)
    pltpu.make_async_copy(recv.at[pl.ds(0, TEAMS - 1)], recv.at[pl.ds(0, TEAMS - 1)], recv_sem).wait()
    pltpu.make_async_copy(recv.at[pl.ds(0, TEAMS - 1)], recv.at[pl.ds(0, TEAMS - 1)], send_sem).wait()
    got = recv[...]
    targets_out[...] = got
    flag_lanes = iota((TEAMS, 128), 1)
    flags = jnp.where((flag_lanes >= 64) & (flag_lanes < 96), got[:, 1, :], 0.0)
    counts = jnp.sum(flags, axis=1, keepdims=True)
    before = jnp.where(iota((TEAMS, 128), 0) < flag_lanes, counts, 0.0)
    offset_out[...] = jnp.sum(before, axis=0, keepdims=True).astype(jnp.int32)


def pair_kernel(offset, targets, field, partial, comp, comp_out, tb, ft, fs, bmat, sum_s, sum_t):
    lane = iota((8, 128), 1)
    sub = iota((8, 128), 0)
    total = offset[0, TEAMS]
    tiles = lax.div(total + 127, 128)

    def clear(tile, carry):
        comp[:, pl.ds(pl.multiple_of(tile * 128, 128), 128)] = jnp.zeros((8, 128), F32)
        return carry

    lax.fori_loop(0, tiles + 2, clear, 0)

    def compact(team, carry):
        start = offset[0, team]
        count = offset[0, team + 1] - start
        message = targets[team]
        rows = jnp.where(sub < 4, message[0:1, :], message[1:2, :])
        rows = fanned(rows, 96)
        rows = jnp.where(lane < count, rows, 0.0)
        shift = lax.rem(start, 128)
        rows = pltpu.roll(rows, shift, 1)
        first = pl.multiple_of(lax.div(start, 128) * 128, 128)
        comp[:, pl.ds(first, 128)] += jnp.where(lane >= shift, rows, 0.0)
        comp[:, pl.ds(first + 128, 128)] += jnp.where(lane < shift, rows, 0.0)
        return carry

    lax.fori_loop(0, TEAMS, compact, 0)

    def target_tile(tile, carry):
        at = pl.multiple_of(tile * 128, 128)
        rows = comp[:, pl.ds(at, 128)]
        for k in range(3):
            tb[k, pl.ds(at, 128), :] = jnp.transpose(jnp.broadcast_to(rows[k : k + 1, :], (128, 128)))
        inner = rows[0:1] * rows[3:4] + rows[1:2] * rows[4:5] + rows[2:3] * rows[5:6]
        y = jnp.concatenate([-rows[3:6], -rows[0:3], jnp.ones((1, 128), F32), inner], 0)
        a, b, c = (part.astype(F32) for part in split3(y))
        stack = jnp.concatenate([a, b, a, b, c, a, jnp.zeros((80, 128), F32)], 0)
        ft[pl.ds(at, 128), :] = jnp.transpose(stack).astype(BF16)
        return carry

    lax.fori_loop(0, tiles, target_tile, 0)

    def source_tile(tile, carry):
        at = pl.multiple_of(tile * 128, 128)
        rows = field[:, pl.ds(at, 128)]
        inner = rows[0:1] * rows[3:4] + rows[1:2] * rows[4:5] + rows[2:3] * rows[5:6]
        x = jnp.concatenate([rows[0:6], inner, jnp.ones((1, 128), F32)], 0)
        a, b, c = (part.astype(F32) for part in split3(x))
        stack = jnp.concatenate([a, a, b, b, a, c, jnp.zeros((80, 128), F32)], 0)
        fs[:, pl.ds(at, 128)] = stack.astype(BF16)
        weighted = jnp.where(sub < 6, rows * rows[6:7, :], rows)
        a, b, c = (part.astype(F32) for part in split3(weighted))
        stack = jnp.concatenate([a, b, c, jnp.zeros((104, 128), F32)], 0)
        bmat[pl.ds(at, 128), :] = jnp.transpose(stack).astype(BF16)
        return carry

    lax.fori_loop(0, STARS_DEV // 128, source_tile, 0)

    def block(number, carry):
        at = pl.multiple_of(number * TB, TB)

        def chunk(step, sums):
            base = pl.multiple_of(step * CHUNK, CHUNK)
            twist = jnp.dot(ft[pl.ds(at, TB), :], fs[:, pl.ds(base, CHUNK)], preferred_element_type=F32)
            left = []
            for k in range(CHUNK // 256):
                parts = [[], [], [], []]
                for g in range(TB // 16):
                    halves = []
                    for m in range(2):
                        cols = pl.ds(base + k * 256 + m * 128, 128)
                        d = [field[c : c + 1, cols] - tb[c, pl.ds(at + g * 16, 16), :] for c in range(3)]
                        r2 = d[0] * d[0] + d[1] * d[1] + d[2] * d[2] + SOFTENING
                        q = lax.rsqrt(r2)
                        q2 = q * q
                        s = q * q2
                        u = twist[g * 16 : g * 16 + 16, k * 256 + m * 128 : k * 256 + m * 128 + 128]
                        t = (u * q2) * s
                        s_hi, t_hi = s.astype(BF16), t.astype(BF16)
                        s_lo = (s - s_hi.astype(F32)).astype(BF16)
                        t_lo = (t - t_hi.astype(F32)).astype(BF16)
                        halves.append((s_hi, t_hi, s_lo, t_lo))
                    for n in range(4):
                        parts[n].append(jnp.concatenate([halves[0][n], halves[1][n]], 1))
                hi = jnp.concatenate(parts[0] + parts[1], 0)
                lo = jnp.concatenate(parts[2] + parts[3], 0)
                left += [hi, lo]
            right = []
            for k in range(CHUNK // 256):
                b = bmat[pl.ds(base + k * 256, 256), :]
                right += [b, b]
            out = jnp.dot(
                jnp.concatenate(left, 1), jnp.concatenate(right, 0), preferred_element_type=F32
            )
            return sums + out

        sums = lax.fori_loop(0, STARS_DEV // CHUNK, chunk, jnp.zeros((2 * TB, 128), F32))
        sum_s[pl.ds(at, TB), :] = sums[:TB]
        sum_t[pl.ds(at, TB), :] = sums[TB:]
        return carry

    lax.fori_loop(0, lax.div(total + TB - 1, TB), block, 0)

    def result_tile(tile, carry):
        at = pl.multiple_of(tile * 128, 128)
        rows = comp[:, pl.ds(at, 128)]

        def folded(ref):
            cols = jnp.transpose(ref[pl.ds(at, 128), :])
            part = cols[0:8] + cols[8:16] + cols[16:24]
            return part - rows * part[6:7, :]

        g_s, g_t = folded(sum_s), folded(sum_t)
        g_t = pltpu.roll(g_t, 3, 0)
        out = jnp.where((sub >= 3) & (sub < 6), g_s - 3.0 * g_t, g_s)
        comp_out[:, pl.ds(at, 128)] = jnp.where(sub < 6, out, 0.0)
        return carry

    lax.fori_loop(0, tiles, result_tile, 0)

    def expand(team, carry):
        start = offset[0, team]
        count = offset[0, team + 1] - start
        shift = lax.rem(start, 128)
        first = pl.multiple_of(lax.div(start, 128) * 128, 128)
        both = jnp.where(lane >= shift, comp_out[:, pl.ds(first, 128)], comp_out[:, pl.ds(first + 128, 128)])
        rows = pltpu.roll(both, lax.rem(128 - shift, 128), 1)
        rows = jnp.where(lane < count, rows, 0.0)
        rows = fanned(rows, 32)
        rows = jnp.where(lane // 32 == lax.rem(sub, 4), rows, 0.0)
        partial[team] = jnp.concatenate(
            [jnp.sum(rows[0:4], axis=0, keepdims=True), jnp.sum(rows[4:8], axis=0, keepdims=True)], 0
        )
        return carry

    lax.fori_loop(0, TEAMS, expand, 0)


def total_kernel(partial, live, force, new_jerk, recv, mine, ring, send_sem, recv_sem, send_sem2, recv_sem2):
    team = lax.axis_index("blk")
    rep = lax.axis_index("rep")
    barrier = pltpu.get_barrier_semaphore()
    signal_peers(barrier, "blk", team, TEAMS)
    signal_peers(barrier, "rep", rep, REPS)
    phase = phase_of(team, rep)
    recv[team] = partial[team]
    source = iota((CAP, CAP), 0)
    slot = iota((CAP, CAP), 1)
    place = jnp.where(slot == lax.rem(source, SHARE) * REPS + source // SHARE, 1.0, 0.0).astype(BF16)
    pl.semaphore_wait(barrier, TEAMS + REPS - 2)

    def send(step, carry):
        peer = lax.rem(team + step, TEAMS)
        pltpu.make_async_remote_copy(
            src_ref=partial.at[peer],
            dst_ref=recv.at[team],
            send_sem=send_sem,
            recv_sem=recv_sem,
            device_id={"blk": peer},
            device_id_type=MESH,
        ).start()
        return carry

    lax.fori_loop(1, TEAMS, send, 0)
    pltpu.make_async_copy(recv.at[pl.ds(0, TEAMS - 1)], recv.at[pl.ds(0, TEAMS - 1)], recv_sem).wait()
    summed = jnp.sum(recv[...], axis=0)
    mine[...] = summed
    ring[phase] = summed

    def pass_on(step, carry):
        pltpu.make_async_remote_copy(
            src_ref=mine,
            dst_ref=ring.at[phase],
            send_sem=send_sem2,
            recv_sem=recv_sem2,
            device_id={"rep": lax.rem(rep + step, REPS)},
            device_id_type=MESH,
        ).start()
        return carry

    lax.fori_loop(1, REPS, pass_on, 0)
    pltpu.make_async_copy(recv.at[pl.ds(0, TEAMS - 1)], recv.at[pl.ds(0, TEAMS - 1)], send_sem).wait()
    pltpu.make_async_copy(ring.at[pl.ds(0, REPS - 1)], ring.at[pl.ds(0, REPS - 1)], recv_sem2).wait()
    pltpu.make_async_copy(ring.at[pl.ds(0, REPS - 1)], ring.at[pl.ds(0, REPS - 1)], send_sem2).wait()
    lane = iota((8, 128), 1)
    sub = iota((8, 128), 0)
    halves = []
    for half in range(2):
        tile = jnp.zeros((8, 128), F32)
        for k in range(4):
            message = ring[half * 4 + k]
            rows = jnp.where(sub < 4, message[0:1, :], message[1:2, :])
            rows = fanned(rows, 96)
            rows = rows if k == 0 else pltpu.roll(rows, 32 * k, 1)
            tile = jnp.where(lane // 32 == k, rows, tile)
        halves.append(tile)
    x = jnp.concatenate(halves, 1)
    a, b, c = (part.astype(F32) for part in split3(x))
    stack = jnp.concatenate([a, b, c, jnp.zeros((8, CAP), F32)], 0).astype(BF16)
    moved = jnp.dot(stack, place, preferred_element_type=F32)
    sums = moved[0:8] + moved[8:16] + moved[16:24]
    scaled = jnp.where(live[...] >= 0, sums / (STARS_DEV * TEAMS), 0.0)
    force[...] = scaled[0:3]
    new_jerk[...] = scaled[3:6]


def in_vmem():
    return pl.BlockSpec(memory_space=pltpu.VMEM)


def in_smem():
    return pl.BlockSpec(memory_space=pltpu.SMEM)


def body(position, velocity, accel, jerk, mass, elapsed, active_index):
    shape = jax.ShapeDtypeStruct
    message = pltpu.VMEM((TEAMS, 2, 128), F32)
    dma = pltpu.SemaphoreType.DMA
    own, field = pl.pallas_call(
        predict_kernel,
        out_shape=(shape((2, 128), F32), shape((8, STARS_DEV), F32)),
        in_specs=[in_smem()] + [in_vmem()] * 6,
        out_specs=(in_vmem(),) * 2,
        name="predict",
    )(active_index, position, velocity, accel, jerk, mass[None, :], elapsed[None, :])
    targets, offset = pl.pallas_call(
        share_kernel,
        out_shape=(shape((TEAMS, 2, 128), F32), shape((1, 128), jnp.int32)),
        in_specs=[in_vmem()],
        out_specs=(in_vmem(),) * 2,
        scratch_shapes=[message, dma, dma],
        compiler_params=pltpu.CompilerParams(collective_id=0, has_side_effects=True),
        name="share",
    )(own)
    partial = pl.pallas_call(
        pair_kernel,
        out_shape=shape((TEAMS, 2, 128), F32),
        in_specs=[in_smem(), in_vmem(), in_vmem()],
        out_specs=in_vmem(),
        scratch_shapes=[
            pltpu.VMEM((8, MAX_ROWS + 256), F32),
            pltpu.VMEM((8, MAX_ROWS + 256), F32),
            pltpu.VMEM((3, MAX_ROWS, 128), F32),
            pltpu.VMEM((MAX_ROWS, 128), BF16),
            pltpu.VMEM((128, STARS_DEV), BF16),
            pltpu.VMEM((STARS_DEV, 128), BF16),
            pltpu.VMEM((MAX_ROWS, 128), F32),
            pltpu.VMEM((MAX_ROWS, 128), F32),
        ],
        compiler_params=pltpu.CompilerParams(vmem_limit_bytes=48 * 2**20),
        name="pairs",
    )(offset, targets, field)
    return pl.pallas_call(
        total_kernel,
        out_shape=(shape((3, CAP), F32), shape((3, CAP), F32)),
        in_specs=[in_vmem(), in_vmem()],
        out_specs=(in_vmem(),) * 2,
        scratch_shapes=[message, pltpu.VMEM((2, 128), F32), pltpu.VMEM((REPS, 2, 128), F32), dma, dma, dma, dma],
        compiler_params=pltpu.CompilerParams(collective_id=1, has_side_effects=True),
        name="totals",
    )(partial, active_index[None, :])


def solution(mesh):
    in_specs = (
        P(None, "blk"),
        P(None, "blk"),
        P(None, "blk"),
        P(None, "blk"),
        P("blk"),
        P("blk"),
        P("blk"),
    )
    out_specs = (P(None, "blk"), P(None, "blk"))
    return jax.shard_map(body, mesh=mesh, in_specs=in_specs, out_specs=out_specs, check_vma=False)
```

```python
import functools

import jax
import jax.numpy as jnp
from jax import lax
from jax.experimental import pallas as pl
from jax.experimental.pallas import tpu as pltpu
from jax.sharding import PartitionSpec as P

SOFTENING = 0.001
MESH = pl.DeviceIdType.MESH
F32 = jnp.float32
BF16 = jnp.bfloat16
TEAMS = 64
REPS = 8
CAP = 256
SHARE = CAP // REPS
STARS_DEV = 8192
MAX_ROWS = TEAMS * SHARE
TB = 64
GROUP = 16
UNROLL = 8


def iota(shape, dim):
    return lax.broadcasted_iota(jnp.int32, shape, dim)


def phase_of(team, rep):
    return lax.rem(rep + 3 * team, REPS)


def split3(x):
    a = x.astype(BF16)
    rest = x - a.astype(F32)
    b = rest.astype(BF16)
    c = (rest - b.astype(F32)).astype(BF16)
    return a, b, c


def fanned(rows, unit):
    sub = lax.rem(iota((8, 128), 0), 4)
    out = rows
    for k in range(1, 4):
        out = jnp.where(sub == k, pltpu.roll(rows, unit * k % 128, 1), out)
    return out


def signal_peers(barrier, axis, me, size):
    def one(step, carry):
        pl.semaphore_signal(
            barrier, inc=1, device_id={axis: lax.rem(me + step, size)}, device_id_type=MESH
        )
        return carry

    lax.fori_loop(1, size, one, 0)


def predict_kernel(index_ref, pos, vel, acc, jrk, mass, elapsed, own, field):
    team = lax.axis_index("blk")
    rep = lax.axis_index("rep")
    h = elapsed[...]
    v, a, j = vel[...], acc[...], jrk[...]
    field[0:3, :] = pos[...] + h * (v + h * (0.5 * a + h / 6.0 * j))
    field[3:6, :] = v + h * (a + 0.5 * h * j)
    field[6:7, :] = jnp.ones((1, STARS_DEV), F32)
    field[7:8, :] = jnp.zeros((1, STARS_DEV), F32)

    phase = phase_of(team, rep)
    lane = iota((8, 128), 1)
    sub = iota((8, 128), 0)
    picked = jnp.zeros((8, 128), F32)
    for k in range(SHARE):
        index = index_ref[REPS * k + phase]
        local = jnp.clip(index - team * STARS_DEV, 0, STARS_DEV - 1)
        tile = field[:, pl.ds(pl.multiple_of(lax.div(local, 128) * 128, 128), 128)]
        turned = pltpu.roll(tile, lax.rem(k - lax.rem(local, 128) + 128, 128), 1)
        picked = jnp.where((lane == k) & (index >= 0), turned, picked)
    spread = fanned(picked, 32)
    spread = jnp.where(lane // 32 == lax.rem(sub, 4), spread, 0.0)
    own[...] = jnp.concatenate(
        [jnp.sum(spread[0:4], axis=0, keepdims=True), jnp.sum(spread[4:8], axis=0, keepdims=True)], 0
    )
    field[6:7, :] = mass[...]


def share_kernel(own, targets_out, offset_out, recv, send_sem, recv_sem):
    team = lax.axis_index("blk")
    barrier = pltpu.get_barrier_semaphore()
    signal_peers(barrier, "blk", team, TEAMS)
    recv[team] = own[...]
    pl.semaphore_wait(barrier, TEAMS - 1)

    def send(step, carry):
        pltpu.make_async_remote_copy(
            src_ref=own,
            dst_ref=recv.at[team],
            send_sem=send_sem,
            recv_sem=recv_sem,
            device_id={"blk": lax.rem(team + step, TEAMS)},
            device_id_type=MESH,
        ).start()
        return carry

    lax.fori_loop(1, TEAMS, send, 0)
    pltpu.make_async_copy(recv.at[pl.ds(0, TEAMS - 1)], recv.at[pl.ds(0, TEAMS - 1)], recv_sem).wait()
    pltpu.make_async_copy(recv.at[pl.ds(0, TEAMS - 1)], recv.at[pl.ds(0, TEAMS - 1)], send_sem).wait()
    got = recv[...]
    targets_out[...] = got
    flag_lanes = iota((TEAMS, 128), 1)
    flags = jnp.where((flag_lanes >= 64) & (flag_lanes < 96), got[:, 1, :], 0.0)
    counts = jnp.sum(flags, axis=1, keepdims=True)
    before = jnp.where(iota((TEAMS, 128), 0) < flag_lanes, counts, 0.0)
    offset_out[...] = jnp.sum(before, axis=0, keepdims=True).astype(jnp.int32)


def pair_kernel(offset, targets, field, partial, comp, comp_out, tb, bmat, sum_s, sum_t):
    lane = iota((8, 128), 1)
    sub = iota((8, 128), 0)
    total = offset[0, TEAMS]
    tiles = lax.div(total + 127, 128)

    def clear(tile, carry):
        comp[:, pl.ds(pl.multiple_of(tile * 128, 128), 128)] = jnp.zeros((8, 128), F32)
        return carry

    lax.fori_loop(0, tiles + 2, clear, 0)

    def compact(step, carry):
        ready = []
        for k in range(UNROLL):
            team = step * UNROLL + k
            start = offset[0, team]
            count = offset[0, team + 1] - start
            message = targets[team]
            rows = jnp.where(sub < 4, message[0:1, :], message[1:2, :])
            rows = jnp.where(lane < count, fanned(rows, 96), 0.0)
            shift = lax.rem(start, 128)
            ready.append((pl.multiple_of(lax.div(start, 128) * 128, 128), shift, pltpu.roll(rows, shift, 1)))
        for first, shift, rows in ready:
            comp[:, pl.ds(first, 128)] += jnp.where(lane >= shift, rows, 0.0)
            comp[:, pl.ds(first + 128, 128)] += jnp.where(lane < shift, rows, 0.0)
        return carry

    lax.fori_loop(0, TEAMS // UNROLL, compact, 0)

    def target_tile(tile, carry):
        at = pl.multiple_of(tile * 128, 128)
        rows = comp[:, pl.ds(at, 128)]
        for k in range(6):
            tb[k, pl.ds(at, 128), :] = jnp.transpose(jnp.broadcast_to(rows[k : k + 1, :], (128, 128)))
        return carry

    lax.fori_loop(0, tiles, target_tile, 0)

    def source_tile(step, carry):
        for k in range(4):
            at = pl.multiple_of(step * 512 + k * 128, 128)
            rows = field[:, pl.ds(at, 128)]
            weighted = jnp.where(sub < 6, rows * rows[6:7, :], rows)
            a, b, c = (part.astype(F32) for part in split3(weighted))
            stack = jnp.concatenate([a, b, c, jnp.zeros((8, 128), F32)], 0)
            bmat[pl.ds(at, 128), 0:32] = jnp.transpose(stack).astype(BF16)
        return carry

    lax.fori_loop(0, STARS_DEV // 512, source_tile, 0)

    def with_accumulators(*accs):
        groups = TB // GROUP
        acc_s = [accs[m * groups : (m + 1) * groups] for m in range(2)]
        acc_t = [accs[(2 + m) * groups : (3 + m) * groups] for m in range(2)]

        def stage(chunk, register):
            for m in range(2):
                cols = pl.ds(pl.multiple_of(chunk * 512 + m * 256, 256), 256)
                pltpu.matmul_push_rhs(bmat[cols, :], register, m)

        def add_chunk(at, chunk, register):
            for g in range(groups):
                rows = pl.ds(at + g * GROUP, GROUP)
                for m in range(2):
                    parts = [[], [], [], []]
                    for half in range(2):
                        cols = pl.ds(pl.multiple_of(chunk * 512 + m * 256 + half * 128, 128), 128)
                        d = [field[c : c + 1, cols] - tb[c, rows, :] for c in range(3)]
                        w = [field[c + 3 : c + 4, cols] - tb[c + 3, rows, :] for c in range(3)]
                        r2 = d[0] * d[0] + d[1] * d[1] + d[2] * d[2] + SOFTENING
                        q = lax.rsqrt(r2)
                        u = d[0] * w[0] + d[1] * w[1] + d[2] * w[2]
                        q2 = q * q
                        s = q * q2
                        t = (u * q2) * s
                        s_hi, t_hi = s.astype(BF16), t.astype(BF16)
                        parts[0].append(s_hi)
                        parts[1].append((s - s_hi.astype(F32)).astype(BF16))
                        parts[2].append(t_hi)
                        parts[3].append((t - t_hi.astype(F32)).astype(BF16))
                    parts = [jnp.concatenate(pair, 1) for pair in parts]
                    first = register if g == 0 else None
                    pltpu.matmul_acc_lhs(acc_s[m][g], parts[0], load_staged_rhs=first)
                    pltpu.matmul_acc_lhs(acc_s[m][g], parts[1])
                    pltpu.matmul_acc_lhs(acc_t[m][g], parts[2])
                    pltpu.matmul_acc_lhs(acc_t[m][g], parts[3])

        chunks = STARS_DEV // 512

        def block(number, carry):
            at = pl.multiple_of(number * TB, TB)
            stage(0, 0)

            def two_chunks(step, inner):
                for k in range(2):
                    chunk = step * 2 + k
                    stage(jnp.minimum(chunk + 1, chunks - 1), 1 - k)
                    add_chunk(at, chunk, k)
                return inner

            lax.fori_loop(0, chunks // 2, two_chunks, 0)
            for g in range(groups):
                rows = pl.ds(at + g * GROUP, GROUP)
                sum_s[rows, :] = pltpu.matmul_pop(acc_s[0][g])[:, :128] + pltpu.matmul_pop(acc_s[1][g])[:, :128]
                sum_t[rows, :] = pltpu.matmul_pop(acc_t[0][g])[:, :128] + pltpu.matmul_pop(acc_t[1][g])[:, :128]
            for m in range(2):
                pltpu.matmul_acc_lhs(acc_s[m][0], jnp.zeros((GROUP, 256), BF16), load_staged_rhs=0)
                pltpu.matmul_pop(acc_s[m][0])
            return carry

        lax.fori_loop(0, lax.div(total + TB - 1, TB), block, 0)

    sets = []
    for m in (0, 1, 0, 1):
        sets += [pltpu.ACC(m)((GROUP, 256), F32)] * (TB // GROUP)
    pl.run_scoped(with_accumulators, *sets)

    def result_tile(tile, carry):
        at = pl.multiple_of(tile * 128, 128)
        rows = comp[:, pl.ds(at, 128)]

        def folded(ref):
            cols = jnp.transpose(ref[pl.ds(at, 128), :])
            part = cols[0:8] + cols[8:16] + cols[16:24]
            return part - rows * part[6:7, :]

        g_s, g_t = folded(sum_s), folded(sum_t)
        g_t = pltpu.roll(g_t, 3, 0)
        out = jnp.where((sub >= 3) & (sub < 6), g_s - 3.0 * g_t, g_s)
        comp_out[:, pl.ds(at, 128)] = jnp.where(sub < 6, out, 0.0)
        return carry

    lax.fori_loop(0, tiles, result_tile, 0)

    def expand(step, carry):
        for k in range(UNROLL):
            team = step * UNROLL + k
            start = offset[0, team]
            count = offset[0, team + 1] - start
            shift = lax.rem(start, 128)
            first = pl.multiple_of(lax.div(start, 128) * 128, 128)
            both = jnp.where(lane >= shift, comp_out[:, pl.ds(first, 128)], comp_out[:, pl.ds(first + 128, 128)])
            rows = pltpu.roll(both, lax.rem(128 - shift, 128), 1)
            rows = fanned(jnp.where(lane < count, rows, 0.0), 32)
            rows = rows + pltpu.roll(rows, 6, 0)
            rows = rows + pltpu.roll(rows, 7, 0)
            partial[team, 0:1, :] = rows[0:1, :]
            partial[team, 1:2, :] = rows[4:5, :]
        return carry

    lax.fori_loop(0, TEAMS // UNROLL, expand, 0)


def total_kernel(partial, live, force, new_jerk, recv, mine, ring, send_sem, recv_sem, send_sem2, recv_sem2):
    team = lax.axis_index("blk")
    rep = lax.axis_index("rep")
    barrier = pltpu.get_barrier_semaphore()
    signal_peers(barrier, "blk", team, TEAMS)
    signal_peers(barrier, "rep", rep, REPS)
    phase = phase_of(team, rep)
    recv[team] = partial[team]
    source = iota((CAP, CAP), 0)
    slot = iota((CAP, CAP), 1)
    place = jnp.where(slot == lax.rem(source, SHARE) * REPS + source // SHARE, 1.0, 0.0).astype(BF16)
    pl.semaphore_wait(barrier, TEAMS + REPS - 2)

    def send(step, carry):
        peer = lax.rem(team + step, TEAMS)
        pltpu.make_async_remote_copy(
            src_ref=partial.at[peer],
            dst_ref=recv.at[team],
            send_sem=send_sem,
            recv_sem=recv_sem,
            device_id={"blk": peer},
            device_id_type=MESH,
        ).start()
        return carry

    lax.fori_loop(1, TEAMS, send, 0)
    pltpu.make_async_copy(recv.at[pl.ds(0, TEAMS - 1)], recv.at[pl.ds(0, TEAMS - 1)], recv_sem).wait()
    summed = jnp.sum(recv[...], axis=0)
    mine[...] = summed
    ring[phase] = summed

    def pass_on(step, carry):
        pltpu.make_async_remote_copy(
            src_ref=mine,
            dst_ref=ring.at[phase],
            send_sem=send_sem2,
            recv_sem=recv_sem2,
            device_id={"rep": lax.rem(rep + step, REPS)},
            device_id_type=MESH,
        ).start()
        return carry

    lax.fori_loop(1, REPS, pass_on, 0)
    pltpu.make_async_copy(recv.at[pl.ds(0, TEAMS - 1)], recv.at[pl.ds(0, TEAMS - 1)], send_sem).wait()
    pltpu.make_async_copy(ring.at[pl.ds(0, REPS - 1)], ring.at[pl.ds(0, REPS - 1)], recv_sem2).wait()
    pltpu.make_async_copy(ring.at[pl.ds(0, REPS - 1)], ring.at[pl.ds(0, REPS - 1)], send_sem2).wait()
    lane = iota((8, 128), 1)
    sub = iota((8, 128), 0)
    halves = []
    for half in range(2):
        tile = jnp.zeros((8, 128), F32)
        for k in range(4):
            message = ring[half * 4 + k]
            rows = jnp.where(sub < 4, message[0:1, :], message[1:2, :])
            rows = fanned(rows, 96)
            rows = rows if k == 0 else pltpu.roll(rows, 32 * k, 1)
            tile = jnp.where(lane // 32 == k, rows, tile)
        halves.append(tile)
    x = jnp.concatenate(halves, 1)
    a, b, c = (part.astype(F32) for part in split3(x))
    stack = jnp.concatenate([a, b, c, jnp.zeros((8, CAP), F32)], 0).astype(BF16)
    moved = jnp.dot(stack, place, preferred_element_type=F32)
    sums = moved[0:8] + moved[8:16] + moved[16:24]
    scaled = jnp.where(live[...] >= 0, sums / (STARS_DEV * TEAMS), 0.0)
    force[...] = scaled[0:3]
    new_jerk[...] = scaled[3:6]


def in_vmem():
    return pl.BlockSpec(memory_space=pltpu.VMEM)


def in_smem():
    return pl.BlockSpec(memory_space=pltpu.SMEM)


def pairs(offset, targets, field):
    shape = jax.ShapeDtypeStruct
    return pl.pallas_call(
        pair_kernel,
        out_shape=shape((TEAMS, 2, 128), F32),
        in_specs=[in_smem(), in_vmem(), in_vmem()],
        out_specs=in_vmem(),
        scratch_shapes=[
            pltpu.VMEM((8, MAX_ROWS + 256), F32),
            pltpu.VMEM((8, MAX_ROWS + 256), F32),
            pltpu.VMEM((6, MAX_ROWS, 128), F32),
            pltpu.VMEM((STARS_DEV, 256), BF16),
            pltpu.VMEM((MAX_ROWS, 128), F32),
            pltpu.VMEM((MAX_ROWS, 128), F32),
        ],
        compiler_params=pltpu.CompilerParams(vmem_limit_bytes=32 * 2**20),
        name="pairs",
    )(offset, targets, field)


def body(position, velocity, accel, jerk, mass, elapsed, active_index):
    shape = jax.ShapeDtypeStruct
    message = pltpu.VMEM((TEAMS, 2, 128), F32)
    dma = pltpu.SemaphoreType.DMA
    own, field = pl.pallas_call(
        predict_kernel,
        out_shape=(shape((2, 128), F32), shape((8, STARS_DEV), F32)),
        in_specs=[in_smem()] + [in_vmem()] * 6,
        out_specs=(in_vmem(),) * 2,
        name="predict",
    )(active_index, position, velocity, accel, jerk, mass[None, :], elapsed[None, :])
    targets, offset = pl.pallas_call(
        share_kernel,
        out_shape=(shape((TEAMS, 2, 128), F32), shape((1, 128), jnp.int32)),
        in_specs=[in_vmem()],
        out_specs=(in_vmem(),) * 2,
        scratch_shapes=[message, dma, dma],
        compiler_params=pltpu.CompilerParams(collective_id=0, has_side_effects=True),
        name="share",
    )(own)
    partial = pairs(offset, targets, field)
    return pl.pallas_call(
        total_kernel,
        out_shape=(shape((3, CAP), F32), shape((3, CAP), F32)),
        in_specs=[in_vmem(), in_vmem()],
        out_specs=(in_vmem(),) * 2,
        scratch_shapes=[message, pltpu.VMEM((2, 128), F32), pltpu.VMEM((REPS, 2, 128), F32), dma, dma, dma, dma],
        compiler_params=pltpu.CompilerParams(collective_id=1, has_side_effects=True),
        name="totals",
    )(partial, active_index[None, :])


def solution(mesh):
    in_specs = (
        P(None, "blk"),
        P(None, "blk"),
        P(None, "blk"),
        P(None, "blk"),
        P("blk"),
        P("blk"),
        P("blk"),
    )
    out_specs = (P(None, "blk"), P(None, "blk"))
    return jax.shard_map(body, mesh=mesh, in_specs=in_specs, out_specs=out_specs, check_vma=False)
```

```python
import functools

import jax
import jax.numpy as jnp
from jax import lax
from jax.experimental import pallas as pl
from jax.experimental.pallas import tpu as pltpu
from jax.sharding import PartitionSpec as P

SOFTENING = 0.001
MESH = pl.DeviceIdType.MESH
F32 = jnp.float32
BF16 = jnp.bfloat16
TEAMS = 64
REPS = 8
CAP = 256
SHARE = CAP // REPS
STARS_DEV = 8192
MAX_ROWS = TEAMS * SHARE
TB = 64
GROUP = 16
UNROLL = 8


def iota(shape, dim):
    return lax.broadcasted_iota(jnp.int32, shape, dim)


def phase_of(team, rep):
    return lax.rem(rep + 3 * team, REPS)


def split3(x):
    a = x.astype(BF16)
    rest = x - a.astype(F32)
    b = rest.astype(BF16)
    c = (rest - b.astype(F32)).astype(BF16)
    return a, b, c


def fanned(rows, unit):
    sub = lax.rem(iota((8, 128), 0), 4)
    out = rows
    for k in range(1, 4):
        out = jnp.where(sub == k, pltpu.roll(rows, unit * k % 128, 1), out)
    return out


def signal_peers(barrier, axis, me, size):
    def one(step, carry):
        pl.semaphore_signal(
            barrier, inc=1, device_id={axis: lax.rem(me + step, size)}, device_id_type=MESH
        )
        return carry

    lax.fori_loop(1, size, one, 0)


def copy_all(pairs, sems):
    copies = [pltpu.make_async_copy(src, dst, sems.at[k]) for k, (src, dst) in enumerate(pairs)]
    for copy in copies:
        copy.start()
    return copies


def share_kernel(
    index_ref,
    pos_hbm,
    vel_hbm,
    acc_hbm,
    jrk_hbm,
    mass_hbm,
    elapsed_hbm,
    targets_out,
    offset_out,
    field_hbm,
    columns_hbm,
    pos,
    vel,
    acc,
    jrk,
    mass,
    elapsed,
    field,
    columns,
    own,
    recv,
    load_sem,
    store_sem,
    send_sem,
    recv_sem,
):
    team = lax.axis_index("blk")
    rep = lax.axis_index("rep")
    barrier = pltpu.get_barrier_semaphore()
    loads = copy_all(
        [(pos_hbm, pos), (vel_hbm, vel), (acc_hbm, acc), (jrk_hbm, jrk), (mass_hbm, mass), (elapsed_hbm, elapsed)],
        load_sem,
    )
    signal_peers(barrier, "blk", team, TEAMS)
    for copy in loads:
        copy.wait()

    h = elapsed[...]
    v, a, j = vel[...], acc[...], jrk[...]
    field[0:3, :] = pos[...] + h * (v + h * (0.5 * a + h / 6.0 * j))
    field[3:6, :] = v + h * (a + 0.5 * h * j)
    field[6:7, :] = mass[...]
    field[7:8, :] = jnp.ones((1, STARS_DEV), F32)
    stores = [pltpu.make_async_copy(field, field_hbm, store_sem.at[0])]
    stores[0].start()

    phase = phase_of(team, rep)
    lane = iota((8, 128), 1)
    sub = iota((8, 128), 0)
    picked = jnp.zeros((8, 128), F32)
    for group in range(2):
        slots = range(group * 16, group * 16 + 16)
        local = [index_ref[REPS * k + phase] - team * STARS_DEV for k in slots]

        def look(step, found):
            for k in range(4):
                at = pl.multiple_of(step * 512 + k * 128, 128)
                tile = field[:, pl.ds(at, 128)]
                number = lane + at
                found = tuple(jnp.where(number == want, tile, old) for want, old in zip(local, found))
            return found

        found = lax.fori_loop(0, STARS_DEV // 512, look, (jnp.zeros((8, 128), F32),) * 16)
        for k, one in zip(slots, found):
            picked = jnp.where(lane == k, jnp.sum(one, axis=1, keepdims=True), picked)
    picked = jnp.where(sub == 6, pltpu.roll(picked, 7, 0), picked)
    spread = fanned(jnp.where(lane < SHARE, picked, 0.0), 32)
    spread = spread + pltpu.roll(spread, 6, 0)
    spread = spread + pltpu.roll(spread, 7, 0)
    own[0:1, :] = spread[0:1, :]
    own[1:2, :] = spread[4:5, :]
    recv[team] = jnp.concatenate([spread[0:1, :], spread[4:5, :]], 0)

    pl.semaphore_wait(barrier, TEAMS - 1)

    def send(step, carry):
        pltpu.make_async_remote_copy(
            src_ref=own,
            dst_ref=recv.at[team],
            send_sem=send_sem,
            recv_sem=recv_sem,
            device_id={"blk": lax.rem(team + step, TEAMS)},
            device_id_type=MESH,
        ).start()
        return carry

    lax.fori_loop(1, TEAMS, send, 0)

    def source_tile(step, carry):
        for k in range(4):
            at = pl.multiple_of(step * 512 + k * 128, 128)
            rows = field[:, pl.ds(at, 128)]
            weighted = jnp.where(sub < 6, rows * rows[6:7, :], rows)
            a, b, c = (part.astype(F32) for part in split3(weighted))
            stack = jnp.concatenate([a, b, c, jnp.zeros((104, 128), F32)], 0)
            columns[pl.ds(at, 128), :] = jnp.transpose(stack).astype(BF16)
        return carry

    lax.fori_loop(0, STARS_DEV // 512, source_tile, 0)
    stores.append(pltpu.make_async_copy(columns, columns_hbm, store_sem.at[1]))
    stores[1].start()
    pltpu.make_async_copy(recv.at[pl.ds(0, TEAMS - 1)], recv.at[pl.ds(0, TEAMS - 1)], recv_sem).wait()
    pltpu.make_async_copy(recv.at[pl.ds(0, TEAMS - 1)], recv.at[pl.ds(0, TEAMS - 1)], send_sem).wait()
    got = recv[...]
    targets_out[...] = got
    flag_lanes = iota((TEAMS, 128), 1)
    flags = jnp.where((flag_lanes >= 64) & (flag_lanes < 96), got[:, 1, :], 0.0)
    counts = jnp.sum(flags, axis=1, keepdims=True)
    before = jnp.where(iota((TEAMS, 128), 0) < flag_lanes, counts, 0.0)
    offset_out[...] = jnp.sum(before, axis=0, keepdims=True).astype(jnp.int32)
    for copy in stores:
        copy.wait()


def pair_kernel(
    offset_hbm, targets_hbm, field_hbm, columns_hbm, partial,
    offset, targets, field, columns, load_sem, comp, comp_out, tb, sum_s, sum_t,
):
    loads = copy_all(
        [(offset_hbm, offset), (targets_hbm, targets), (field_hbm, field), (columns_hbm, columns)], load_sem
    )
    lane = iota((8, 128), 1)
    sub = iota((8, 128), 0)
    loads[0].wait()
    loads[1].wait()
    total = offset[0, TEAMS]
    tiles = lax.div(total + 127, 128)

    def clear(tile, carry):
        comp[:, pl.ds(pl.multiple_of(tile * 128, 128), 128)] = jnp.zeros((8, 128), F32)
        return carry

    lax.fori_loop(0, tiles + 2, clear, 0)

    def compact(step, carry):
        ready = []
        for k in range(UNROLL):
            team = step * UNROLL + k
            start = offset[0, team]
            count = offset[0, team + 1] - start
            message = targets[team]
            rows = jnp.where(sub < 4, message[0:1, :], message[1:2, :])
            rows = jnp.where(lane < count, fanned(rows, 96), 0.0)
            shift = lax.rem(start, 128)
            ready.append((pl.multiple_of(lax.div(start, 128) * 128, 128), shift, pltpu.roll(rows, shift, 1)))
        for first, shift, rows in ready:
            comp[:, pl.ds(first, 128)] += jnp.where(lane >= shift, rows, 0.0)
            comp[:, pl.ds(first + 128, 128)] += jnp.where(lane < shift, rows, 0.0)
        return carry

    lax.fori_loop(0, TEAMS // UNROLL, compact, 0)

    def target_tile(tile, carry):
        at = pl.multiple_of(tile * 128, 128)
        rows = comp[:, pl.ds(at, 128)]
        for k in range(6):
            tb[k, pl.ds(at, 128), :] = jnp.transpose(jnp.broadcast_to(rows[k : k + 1, :], (128, 128)))
        return carry

    lax.fori_loop(0, tiles, target_tile, 0)

    loads[2].wait()
    loads[3].wait()

    def with_accumulators(*accs):
        groups = TB // GROUP
        acc_s = [accs[m * groups : (m + 1) * groups] for m in range(2)]
        acc_t = [accs[(2 + m) * groups : (3 + m) * groups] for m in range(2)]

        def stage(chunk, register):
            for m in range(2):
                cols = pl.ds(pl.multiple_of(chunk * 512 + m * 256, 256), 256)
                rhs = jnp.concatenate([columns[cols, :], jnp.zeros((256, 128), BF16)], 1)
                pltpu.matmul_push_rhs(rhs, register, m)

        def add_chunk(at, chunk, register):
            for g in range(groups):
                rows = pl.ds(at + g * GROUP, GROUP)
                for m in range(2):
                    parts = [[], [], [], []]
                    for half in range(2):
                        cols = pl.ds(pl.multiple_of(chunk * 512 + m * 256 + half * 128, 128), 128)
                        d = [field[c : c + 1, cols] - tb[c, rows, :] for c in range(3)]
                        w = [field[c + 3 : c + 4, cols] - tb[c + 3, rows, :] for c in range(3)]
                        r2 = d[0] * d[0] + d[1] * d[1] + d[2] * d[2] + SOFTENING
                        q = lax.rsqrt(r2)
                        u = d[0] * w[0] + d[1] * w[1] + d[2] * w[2]
                        q2 = q * q
                        s = q * q2
                        t = (u * q2) * s
                        s_hi, t_hi = s.astype(BF16), t.astype(BF16)
                        parts[0].append(s_hi)
                        parts[1].append((s - s_hi.astype(F32)).astype(BF16))
                        parts[2].append(t_hi)
                        parts[3].append((t - t_hi.astype(F32)).astype(BF16))
                    parts = [jnp.concatenate(pair, 1) for pair in parts]
                    first = register if g == 0 else None
                    pltpu.matmul_acc_lhs(acc_s[m][g], parts[0], load_staged_rhs=first)
                    pltpu.matmul_acc_lhs(acc_s[m][g], parts[1])
                    pltpu.matmul_acc_lhs(acc_t[m][g], parts[2])
                    pltpu.matmul_acc_lhs(acc_t[m][g], parts[3])

        chunks = STARS_DEV // 512

        def block(number, carry):
            at = pl.multiple_of(number * TB, TB)
            stage(0, 0)

            def two_chunks(step, inner):
                for k in range(2):
                    chunk = step * 2 + k
                    stage(jnp.minimum(chunk + 1, chunks - 1), 1 - k)
                    add_chunk(at, chunk, k)
                return inner

            lax.fori_loop(0, chunks // 2, two_chunks, 0)
            for g in range(groups):
                rows = pl.ds(at + g * GROUP, GROUP)
                sum_s[rows, :] = pltpu.matmul_pop(acc_s[0][g])[:, :128] + pltpu.matmul_pop(acc_s[1][g])[:, :128]
                sum_t[rows, :] = pltpu.matmul_pop(acc_t[0][g])[:, :128] + pltpu.matmul_pop(acc_t[1][g])[:, :128]
            for m in range(2):
                pltpu.matmul_acc_lhs(acc_s[m][0], jnp.zeros((GROUP, 256), BF16), load_staged_rhs=0)
                pltpu.matmul_pop(acc_s[m][0])
            return carry

        lax.fori_loop(0, lax.div(total + TB - 1, TB), block, 0)

    sets = []
    for m in (0, 1, 0, 1):
        sets += [pltpu.ACC(m)((GROUP, 256), F32)] * (TB // GROUP)
    pl.run_scoped(with_accumulators, *sets)

    def result_tile(tile, carry):
        at = pl.multiple_of(tile * 128, 128)
        rows = comp[:, pl.ds(at, 128)]

        def folded(ref):
            cols = jnp.transpose(ref[pl.ds(at, 128), :])
            part = cols[0:8] + cols[8:16] + cols[16:24]
            return part - rows * part[6:7, :]

        g_s, g_t = folded(sum_s), folded(sum_t)
        g_t = pltpu.roll(g_t, 3, 0)
        out = jnp.where((sub >= 3) & (sub < 6), g_s - 3.0 * g_t, g_s)
        comp_out[:, pl.ds(at, 128)] = jnp.where(sub < 6, out, 0.0)
        return carry

    lax.fori_loop(0, tiles, result_tile, 0)

    def expand(step, carry):
        for k in range(UNROLL):
            team = step * UNROLL + k
            start = offset[0, team]
            count = offset[0, team + 1] - start
            shift = lax.rem(start, 128)
            first = pl.multiple_of(lax.div(start, 128) * 128, 128)
            both = jnp.where(lane >= shift, comp_out[:, pl.ds(first, 128)], comp_out[:, pl.ds(first + 128, 128)])
            rows = pltpu.roll(both, lax.rem(128 - shift, 128), 1)
            rows = fanned(jnp.where(lane < count, rows, 0.0), 32)
            rows = rows + pltpu.roll(rows, 6, 0)
            rows = rows + pltpu.roll(rows, 7, 0)
            partial[team, 0:1, :] = rows[0:1, :]
            partial[team, 1:2, :] = rows[4:5, :]
        return carry

    lax.fori_loop(0, TEAMS // UNROLL, expand, 0)


def total_kernel(
    partial_hbm, ring_out, partial, recv, mine, ring, load_sem, send_sem, recv_sem, send_sem2, recv_sem2
):
    team = lax.axis_index("blk")
    rep = lax.axis_index("rep")
    barrier = pltpu.get_barrier_semaphore()
    load = pltpu.make_async_copy(partial_hbm, partial, load_sem)
    load.start()
    signal_peers(barrier, "blk", team, TEAMS)
    signal_peers(barrier, "rep", rep, REPS)
    phase = phase_of(team, rep)
    load.wait()
    recv[team] = partial[team]
    pl.semaphore_wait(barrier, TEAMS + REPS - 2)

    def send(step, carry):
        peer = lax.rem(team + step, TEAMS)
        pltpu.make_async_remote_copy(
            src_ref=partial.at[peer],
            dst_ref=recv.at[team],
            send_sem=send_sem,
            recv_sem=recv_sem,
            device_id={"blk": peer},
            device_id_type=MESH,
        ).start()
        return carry

    lax.fori_loop(1, TEAMS, send, 0)
    pltpu.make_async_copy(recv.at[pl.ds(0, TEAMS - 1)], recv.at[pl.ds(0, TEAMS - 1)], recv_sem).wait()
    summed = jnp.sum(recv[...], axis=0)
    mine[...] = summed
    ring[phase] = summed

    def pass_on(step, carry):
        pltpu.make_async_remote_copy(
            src_ref=mine,
            dst_ref=ring.at[phase],
            send_sem=send_sem2,
            recv_sem=recv_sem2,
            device_id={"rep": lax.rem(rep + step, REPS)},
            device_id_type=MESH,
        ).start()
        return carry

    lax.fori_loop(1, REPS, pass_on, 0)
    pltpu.make_async_copy(recv.at[pl.ds(0, TEAMS - 1)], recv.at[pl.ds(0, TEAMS - 1)], send_sem).wait()
    pltpu.make_async_copy(ring.at[pl.ds(0, REPS - 1)], ring.at[pl.ds(0, REPS - 1)], recv_sem2).wait()
    pltpu.make_async_copy(ring.at[pl.ds(0, REPS - 1)], ring.at[pl.ds(0, REPS - 1)], send_sem2).wait()
    ring_out[...] = ring[...]


def finish_kernel(ring, live, force, new_jerk):
    source = iota((CAP, CAP), 0)
    slot = iota((CAP, CAP), 1)
    place = jnp.where(slot == lax.rem(source, SHARE) * REPS + lax.div(source, SHARE), 1.0, 0.0).astype(BF16)
    lane = iota((8, 128), 1)
    sub = iota((8, 128), 0)
    halves = []
    for half in range(2):
        tile = jnp.zeros((8, 128), F32)
        for k in range(4):
            message = ring[half * 4 + k]
            rows = jnp.where(sub < 4, message[0:1, :], message[1:2, :])
            rows = fanned(rows, 96)
            rows = rows if k == 0 else pltpu.roll(rows, 32 * k, 1)
            tile = jnp.where(lane // 32 == k, rows, tile)
        halves.append(tile)
    x = jnp.concatenate(halves, 1)
    a, b, c = (part.astype(F32) for part in split3(x))
    stack = jnp.concatenate([a, b, c, jnp.zeros((8, CAP), F32)], 0).astype(BF16)
    moved = jnp.dot(stack, place, preferred_element_type=F32)
    sums = moved[0:8] + moved[8:16] + moved[16:24]
    scaled = jnp.where(live[...] >= 0, sums / (STARS_DEV * TEAMS), 0.0)
    force[...] = scaled[0:3]
    new_jerk[...] = scaled[3:6]


def in_vmem():
    return pl.BlockSpec(memory_space=pltpu.VMEM)


def in_smem():
    return pl.BlockSpec(memory_space=pltpu.SMEM)


def anywhere():
    return pl.BlockSpec(memory_space=pl.ANY)


def pairs(offset, targets, field, columns):
    return pl.pallas_call(
        pair_kernel,
        out_shape=jax.ShapeDtypeStruct((TEAMS, 2, 128), F32),
        in_specs=[anywhere()] * 4,
        out_specs=in_vmem(),
        scratch_shapes=[
            pltpu.SMEM((1, 128), jnp.int32),
            pltpu.VMEM((TEAMS, 2, 128), F32),
            pltpu.VMEM((8, STARS_DEV), F32),
            pltpu.VMEM((STARS_DEV, 128), BF16),
            pltpu.SemaphoreType.DMA((4,)),
            pltpu.VMEM((8, MAX_ROWS + 256), F32),
            pltpu.VMEM((8, MAX_ROWS + 256), F32),
            pltpu.VMEM((6, MAX_ROWS, 128), F32),
            pltpu.VMEM((MAX_ROWS, 128), F32),
            pltpu.VMEM((MAX_ROWS, 128), F32),
        ],
        compiler_params=pltpu.CompilerParams(vmem_limit_bytes=56 * 2**20),
        name="pairs",
    )(offset, targets, field, columns)


def body(position, velocity, accel, jerk, mass, elapsed, active_index):
    shape = jax.ShapeDtypeStruct
    message = pltpu.VMEM((TEAMS, 2, 128), F32)
    row = pltpu.VMEM((1, STARS_DEV), F32)
    triple = pltpu.VMEM((3, STARS_DEV), F32)
    dma = pltpu.SemaphoreType.DMA
    targets, offset, field, columns = pl.pallas_call(
        share_kernel,
        out_shape=(
            shape((TEAMS, 2, 128), F32),
            shape((1, 128), jnp.int32),
            shape((8, STARS_DEV), F32),
            shape((STARS_DEV, 128), BF16),
        ),
        in_specs=[in_smem()] + [anywhere()] * 6,
        out_specs=(in_vmem(), in_vmem(), anywhere(), anywhere()),
        scratch_shapes=[triple] * 4
        + [row] * 2
        + [
            pltpu.VMEM((8, STARS_DEV), F32),
            pltpu.VMEM((STARS_DEV, 128), BF16),
            pltpu.VMEM((2, 128), F32),
            message,
            dma((6,)),
            dma((2,)),
            dma,
            dma,
        ],
        compiler_params=pltpu.CompilerParams(collective_id=0, has_side_effects=True, vmem_limit_bytes=56 * 2**20),
        name="share",
    )(active_index, position, velocity, accel, jerk, mass[None, :], elapsed[None, :])
    partial = pairs(offset, targets, field, columns)
    ring = pl.pallas_call(
        total_kernel,
        out_shape=shape((REPS, 2, 128), F32),
        in_specs=[anywhere()],
        out_specs=in_vmem(),
        scratch_shapes=[
            message,
            message,
            pltpu.VMEM((2, 128), F32),
            pltpu.VMEM((REPS, 2, 128), F32),
            dma,
            dma,
            dma,
            dma,
            dma,
        ],
        compiler_params=pltpu.CompilerParams(collective_id=1, has_side_effects=True),
        name="totals",
    )(partial)
    return pl.pallas_call(
        finish_kernel,
        out_shape=(shape((3, CAP), F32), shape((3, CAP), F32)),
        in_specs=[in_vmem(), in_vmem()],
        out_specs=(in_vmem(),) * 2,
        name="finish",
    )(ring, active_index[None, :])


def solution(mesh):
    in_specs = (
        P(None, "blk"),
        P(None, "blk"),
        P(None, "blk"),
        P(None, "blk"),
        P("blk"),
        P("blk"),
        P("blk"),
    )
    out_specs = (P(None, "blk"), P(None, "blk"))
    return jax.shard_map(body, mesh=mesh, in_specs=in_specs, out_specs=out_specs, check_vma=False)
```

```python
import functools

import jax
import jax.numpy as jnp
from jax import lax
from jax.experimental import pallas as pl
from jax.experimental.pallas import tpu as pltpu
from jax.sharding import PartitionSpec as P

SOFTENING = 0.001
MESH = pl.DeviceIdType.MESH
F32 = jnp.float32
BF16 = jnp.bfloat16
TEAMS = 64
REPS = 8
CAP = 256
SHARE = CAP // REPS
Z = 8
Y_LOW = 2
PLANE = TEAMS // Y_LOW
STARS_DEV = 8192
MAX_ROWS = TEAMS * SHARE
GROUP = 16
UNROLL = 32


def iota(shape, dim):
    return lax.broadcasted_iota(jnp.int32, shape, dim)


def phase_of(team, rep):
    return lax.rem(rep + 3 * team, REPS)


def split3(x):
    a = x.astype(BF16)
    rest = x - a.astype(F32)
    b = rest.astype(BF16)
    c = (rest - b.astype(F32)).astype(BF16)
    return a, b, c


def fanned(rows, unit):
    sub = lax.rem(iota((8, 128), 0), 4)
    out = rows
    for k in range(1, 4):
        out = jnp.where(sub == k, pltpu.roll(rows, unit * k % 128, 1), out)
    return out


def signal_peers(barrier, axis, me, size):
    def one(step, carry):
        pl.semaphore_signal(
            barrier, inc=1, device_id={axis: lax.rem(me + step, size)}, device_id_type=MESH
        )
        return carry

    lax.fori_loop(1, size, one, 0)


def copy_all(pairs, sems):
    copies = [pltpu.make_async_copy(src, dst, sems.at[k]) for k, (src, dst) in enumerate(pairs)]
    for copy in copies:
        copy.start()
    return copies


def share_kernel(
    index_ref,
    pos_hbm,
    vel_hbm,
    acc_hbm,
    jrk_hbm,
    mass_hbm,
    elapsed_hbm,
    targets_out,
    offset_out,
    field_hbm,
    columns_hbm,
    pos,
    vel,
    acc,
    jrk,
    mass,
    elapsed,
    field,
    columns,
    own,
    recv,
    load_sem,
    store_sem,
    send_sem,
    recv_sem,
):
    team = lax.axis_index("blk")
    rep = lax.axis_index("rep")
    barrier = pltpu.get_barrier_semaphore()
    loads = copy_all(
        [(pos_hbm, pos), (vel_hbm, vel), (acc_hbm, acc), (jrk_hbm, jrk), (mass_hbm, mass), (elapsed_hbm, elapsed)],
        load_sem,
    )
    signal_peers(barrier, "blk", team, TEAMS)
    for copy in loads:
        copy.wait()

    h = elapsed[...]
    v, a, j = vel[...], acc[...], jrk[...]
    field[0:3, :] = pos[...] + h * (v + h * (0.5 * a + h / 6.0 * j))
    field[3:6, :] = v + h * (a + 0.5 * h * j)
    field[6:7, :] = mass[...]
    field[7:8, :] = jnp.ones((1, STARS_DEV), F32)
    stores = [pltpu.make_async_copy(field, field_hbm, store_sem.at[0])]
    stores[0].start()

    phase = phase_of(team, rep)
    lane = iota((8, 128), 1)
    sub = iota((8, 128), 0)
    picked = jnp.zeros((8, 128), F32)
    for group in range(2):
        slots = range(group * 16, group * 16 + 16)
        local = [index_ref[REPS * k + phase] - team * STARS_DEV for k in slots]

        def look(step, found):
            for k in range(4):
                at = pl.multiple_of(step * 512 + k * 128, 128)
                tile = field[:, pl.ds(at, 128)]
                number = lane + at
                found = tuple(jnp.where(number == want, tile, old) for want, old in zip(local, found))
            return found

        found = lax.fori_loop(0, STARS_DEV // 512, look, (jnp.zeros((8, 128), F32),) * 16)
        for k, one in zip(slots, found):
            picked = jnp.where(lane == k, jnp.sum(one, axis=1, keepdims=True), picked)
    picked = jnp.where(sub == 6, pltpu.roll(picked, 7, 0), picked)
    spread = fanned(jnp.where(lane < SHARE, picked, 0.0), 32)
    spread = spread + pltpu.roll(spread, 6, 0)
    spread = spread + pltpu.roll(spread, 7, 0)
    own[0:1, :] = spread[0:1, :]
    own[1:2, :] = spread[4:5, :]
    recv[team] = jnp.concatenate([spread[0:1, :], spread[4:5, :]], 0)

    pl.semaphore_wait(barrier, TEAMS - 1)

    def send(step, carry):
        pltpu.make_async_remote_copy(
            src_ref=own,
            dst_ref=recv.at[team],
            send_sem=send_sem,
            recv_sem=recv_sem,
            device_id={"blk": lax.rem(team + step, TEAMS)},
            device_id_type=MESH,
        ).start()
        return carry

    lax.fori_loop(1, TEAMS, send, 0)

    def source_tile(step, carry):
        for k in range(4):
            at = pl.multiple_of(step * 512 + k * 128, 128)
            rows = field[:, pl.ds(at, 128)]
            weighted = jnp.where(sub < 6, rows * rows[6:7, :], rows)
            a, b, c = (part.astype(F32) for part in split3(weighted))
            stack = jnp.concatenate([a, b, c, jnp.zeros((104, 128), F32)], 0)
            columns[pl.ds(at, 128), :] = jnp.transpose(stack).astype(BF16)
        return carry

    lax.fori_loop(0, STARS_DEV // 512, source_tile, 0)
    stores.append(pltpu.make_async_copy(columns, columns_hbm, store_sem.at[1]))
    stores[1].start()
    pltpu.make_async_copy(recv.at[pl.ds(0, TEAMS - 1)], recv.at[pl.ds(0, TEAMS - 1)], recv_sem).wait()
    pltpu.make_async_copy(recv.at[pl.ds(0, TEAMS - 1)], recv.at[pl.ds(0, TEAMS - 1)], send_sem).wait()
    got = recv[...]
    targets_out[...] = got
    flag_lanes = iota((TEAMS, 128), 1)
    flags = jnp.where((flag_lanes >= 64) & (flag_lanes < 96), got[:, 1, :], 0.0)
    counts = jnp.sum(flags, axis=1, keepdims=True)
    before = jnp.where(iota((TEAMS, 128), 0) < flag_lanes, counts, 0.0)
    offset_out[...] = jnp.sum(before, axis=0, keepdims=True).astype(jnp.int32)
    for copy in stores:
        copy.wait()


def pair_kernel(
    offset_hbm, targets_hbm, field_hbm, columns_hbm, sums_out,
    offset, targets, field, columns, load_sem, comp, tb, sum_s, sum_t,
):
    loads = copy_all(
        [(offset_hbm, offset), (targets_hbm, targets), (field_hbm, field), (columns_hbm, columns)], load_sem
    )
    lane = iota((8, 128), 1)
    sub = iota((8, 128), 0)
    loads[0].wait()
    loads[1].wait()
    total = offset[0, TEAMS]
    tiles = lax.div(total + 127, 128)

    def clear(tile, carry):
        comp[:, pl.ds(pl.multiple_of(tile * 128, 128), 128)] = jnp.zeros((8, 128), F32)
        return carry

    lax.fori_loop(0, tiles + 2, clear, 0)

    def compact(step, carry):
        ready = []
        for k in range(UNROLL):
            team = step * UNROLL + k
            start = offset[0, team]
            count = offset[0, team + 1] - start
            message = targets[team]
            rows = jnp.where(sub < 4, message[0:1, :], message[1:2, :])
            rows = jnp.where(lane < count, fanned(rows, 96), 0.0)
            shift = lax.rem(start, 128)
            ready.append((pl.multiple_of(lax.div(start, 128) * 128, 128), shift, pltpu.roll(rows, shift, 1)))
        for first, shift, rows in ready:
            comp[:, pl.ds(first, 128)] += jnp.where(lane >= shift, rows, 0.0)
            comp[:, pl.ds(first + 128, 128)] += jnp.where(lane < shift, rows, 0.0)
        return carry

    lax.fori_loop(0, TEAMS // UNROLL, compact, 0)

    def target_tile(tile, carry):
        at = pl.multiple_of(tile * 128, 128)
        rows = comp[:, pl.ds(at, 128)]
        for k in range(6):
            tb[k, pl.ds(at, 128), :] = jnp.transpose(jnp.broadcast_to(rows[k : k + 1, :], (128, 128)))
        return carry

    lax.fori_loop(0, tiles, target_tile, 0)

    loads[2].wait()
    loads[3].wait()

    chunks = STARS_DEV // 512

    def stage(chunk, register):
        for m in range(2):
            cols = pl.ds(pl.multiple_of(chunk * 512 + m * 256, 256), 256)
            rhs = jnp.concatenate([columns[cols, :], jnp.zeros((256, 128), BF16)], 1)
            pltpu.matmul_push_rhs(rhs, register, m)

    def add_chunk(at, chunk, register, acc_s, acc_t):
        for g in range(len(acc_s[0])):
            rows = pl.ds(at + g * GROUP, GROUP)
            for m in range(2):
                parts = [[], [], [], []]
                for half in range(2):
                    cols = pl.ds(pl.multiple_of(chunk * 512 + m * 256 + half * 128, 128), 128)
                    d = [field[c : c + 1, cols] - tb[c, rows, :] for c in range(3)]
                    w = [field[c + 3 : c + 4, cols] - tb[c + 3, rows, :] for c in range(3)]
                    r2 = d[0] * d[0] + d[1] * d[1] + d[2] * d[2] + SOFTENING
                    q = lax.rsqrt(r2)
                    u = d[0] * w[0] + d[1] * w[1] + d[2] * w[2]
                    q2 = q * q
                    s = q * q2
                    t = (u * q2) * s
                    s_hi, t_hi = s.astype(BF16), t.astype(BF16)
                    parts[0].append(s_hi)
                    parts[1].append((s - s_hi.astype(F32)).astype(BF16))
                    parts[2].append(t_hi)
                    parts[3].append((t - t_hi.astype(F32)).astype(BF16))
                parts = [jnp.concatenate(pair, 1) for pair in parts]
                first = register if g == 0 else None
                pltpu.matmul_acc_lhs(acc_s[m][g], parts[0], load_staged_rhs=first)
                pltpu.matmul_acc_lhs(acc_s[m][g], parts[1])
                pltpu.matmul_acc_lhs(acc_t[m][g], parts[2])
                pltpu.matmul_acc_lhs(acc_t[m][g], parts[3])

    def add_blocks(size, base, count, unroll):
        groups = size // GROUP

        def scoped(*accs):
            acc_s = [accs[m * groups : (m + 1) * groups] for m in range(2)]
            acc_t = [accs[(2 + m) * groups : (3 + m) * groups] for m in range(2)]

            def block(number, carry):
                at = pl.multiple_of(base + number * size, 32)
                stage(0, 0)

                def some_chunks(step, inner):
                    for k in range(unroll):
                        chunk = step * unroll + k
                        stage(jnp.minimum(chunk + 1, chunks - 1), 1 - k % 2)
                        add_chunk(at, chunk, k % 2, acc_s, acc_t)
                    return inner

                lax.fori_loop(0, chunks // unroll, some_chunks, 0)
                for g in range(groups):
                    rows = pl.ds(at + g * GROUP, GROUP)
                    sum_s[rows, :] = pltpu.matmul_pop(acc_s[0][g])[:, :128] + pltpu.matmul_pop(acc_s[1][g])[:, :128]
                    sum_t[rows, :] = pltpu.matmul_pop(acc_t[0][g])[:, :128] + pltpu.matmul_pop(acc_t[1][g])[:, :128]
                for m in range(2):
                    pltpu.matmul_acc_lhs(acc_s[m][0], jnp.zeros((GROUP, 256), BF16), load_staged_rhs=0)
                    pltpu.matmul_pop(acc_s[m][0])
                return carry

            lax.fori_loop(0, count, block, 0)

        sets = []
        for m in (0, 1, 0, 1):
            sets += [pltpu.ACC(m)((GROUP, 256), F32)] * groups
        pl.run_scoped(scoped, *sets)

    whole = lax.div(total, 96)
    rest = total - whole * 96
    one = jnp.int32(1)
    none = jnp.int32(0)
    add_blocks(96, 0, whole + jnp.where(rest > 64, one, none), 4)
    add_blocks(64, whole * 96, jnp.where((rest > 32) & (rest <= 64), one, none), 4)
    add_blocks(32, whole * 96, jnp.where((rest > 0) & (rest <= 32), one, none), 4)

    def result_tile(tile, carry):
        at = pl.multiple_of(tile * 128, 128)
        rows = comp[:, pl.ds(at, 128)]

        def folded(ref):
            cols = jnp.transpose(ref[pl.ds(at, 128), :])
            part = cols[0:8] + cols[8:16] + cols[16:24]
            return part - rows * part[6:7, :]

        g_s, g_t = folded(sum_s), folded(sum_t)
        g_t = pltpu.roll(g_t, 3, 0)
        out = jnp.where((sub >= 3) & (sub < 6), g_s - 3.0 * g_t, g_s)
        sums_out[tile] = jnp.where(sub < 6, out, 0.0)
        return carry

    lax.fori_loop(0, tiles, result_tile, 0)


def total_kernel(
    offset, sums_hbm, ring_out, sums, partial, recv, mine, column, load_sem, send_sem, recv_sem, send_sem2, recv_sem2
):
    team = lax.axis_index("blk")
    rep = lax.axis_index("rep")
    depth = lax.rem(team, Z)
    low = lax.rem(lax.div(team, Z), Y_LOW)
    wide = lax.div(team, Z * Y_LOW)
    place = wide * Z + depth
    stack = low * REPS + rep

    def team_of(place, low):
        return (lax.div(place, Z) * Y_LOW + low) * Z + lax.rem(place, Z)

    def plane_peer(step):
        return lax.rem(place + step, PLANE)

    def column_peer(step):
        other = lax.rem(stack + step, Y_LOW * REPS)
        return lax.div(other, REPS), lax.rem(other, REPS)

    barrier = pltpu.get_barrier_semaphore()
    load = pltpu.make_async_copy(sums_hbm, sums, load_sem)
    load.start()

    def greet_plane(step, carry):
        pl.semaphore_signal(
            barrier, inc=1, device_id={"blk": team_of(plane_peer(step), low), "rep": rep}, device_id_type=MESH
        )
        return carry

    def greet_column(step, carry):
        peer_low, peer_rep = column_peer(step)
        pl.semaphore_signal(
            barrier, inc=1, device_id={"blk": team_of(place, peer_low), "rep": peer_rep}, device_id_type=MESH
        )
        return carry

    lax.fori_loop(1, PLANE, greet_plane, 0)
    lax.fori_loop(1, Y_LOW * REPS, greet_column, 0)
    load.wait()

    lane = iota((8, 128), 1)
    for k in range(TEAMS):
        start = offset[0, k]
        count = offset[0, k + 1] - start
        first = lax.div(start, 128)
        shift = lax.rem(start, 128)
        both = jnp.where(lane >= shift, sums[first], sums[first + 1])
        rows = pltpu.roll(both, lax.rem(128 - shift, 128), 1)
        rows = fanned(jnp.where(lane < count, rows, 0.0), 32)
        rows = rows + pltpu.roll(rows, 6, 0)
        rows = rows + pltpu.roll(rows, 7, 0)
        at = k // (Z * Y_LOW) * Z + k % Z
        partial[at, k // Z % Y_LOW, 0:1, :] = rows[0:1, :]
        partial[at, k // Z % Y_LOW, 1:2, :] = rows[4:5, :]

    recv[place] = partial[place]
    pl.semaphore_wait(barrier, PLANE + Y_LOW * REPS - 2)

    def send(step, carry):
        peer = plane_peer(step)
        pltpu.make_async_remote_copy(
            src_ref=partial.at[peer],
            dst_ref=recv.at[place],
            send_sem=send_sem,
            recv_sem=recv_sem,
            device_id={"blk": team_of(peer, low), "rep": rep},
            device_id_type=MESH,
        ).start()
        return carry

    lax.fori_loop(1, PLANE, send, 0)
    pltpu.make_async_copy(recv.at[pl.ds(0, PLANE - 1)], recv.at[pl.ds(0, PLANE - 1)], recv_sem).wait()
    summed = jnp.sum(recv[...], axis=0)
    mine[...] = summed
    column[low, phase_of(team, rep)] = mine[low]

    def pass_on(step, carry):
        peer_low, peer_rep = column_peer(step)
        peer = team_of(place, peer_low)
        pltpu.make_async_remote_copy(
            src_ref=mine.at[peer_low],
            dst_ref=column.at[low, phase_of(peer, rep)],
            send_sem=send_sem2,
            recv_sem=recv_sem2,
            device_id={"blk": peer, "rep": peer_rep},
            device_id_type=MESH,
        ).start()
        return carry

    lax.fori_loop(1, Y_LOW * REPS, pass_on, 0)
    pltpu.make_async_copy(recv.at[pl.ds(0, PLANE - 1)], recv.at[pl.ds(0, PLANE - 1)], send_sem).wait()
    flat = partial.at[pl.ds(0, Y_LOW * REPS - 1), 0]
    pltpu.make_async_copy(flat, flat, recv_sem2).wait()
    pltpu.make_async_copy(flat, flat, send_sem2).wait()
    ring_out[...] = column[0] + column[1]


def finish_kernel(ring, live, force, new_jerk):
    source = iota((CAP, CAP), 0)
    slot = iota((CAP, CAP), 1)
    place = jnp.where(slot == lax.rem(source, SHARE) * REPS + lax.div(source, SHARE), 1.0, 0.0).astype(BF16)
    lane = iota((8, 128), 1)
    sub = iota((8, 128), 0)
    halves = []
    for half in range(2):
        tile = jnp.zeros((8, 128), F32)
        for k in range(4):
            message = ring[half * 4 + k]
            rows = jnp.where(sub < 4, message[0:1, :], message[1:2, :])
            rows = fanned(rows, 96)
            rows = rows if k == 0 else pltpu.roll(rows, 32 * k, 1)
            tile = jnp.where(lane // 32 == k, rows, tile)
        halves.append(tile)
    x = jnp.concatenate(halves, 1)
    a, b, c = (part.astype(F32) for part in split3(x))
    stack = jnp.concatenate([a, b, c, jnp.zeros((8, CAP), F32)], 0).astype(BF16)
    moved = jnp.dot(stack, place, preferred_element_type=F32)
    sums = moved[0:8] + moved[8:16] + moved[16:24]
    scaled = jnp.where(live[...] >= 0, sums / (STARS_DEV * TEAMS), 0.0)
    force[...] = scaled[0:3]
    new_jerk[...] = scaled[3:6]


def in_vmem():
    return pl.BlockSpec(memory_space=pltpu.VMEM)


def in_smem():
    return pl.BlockSpec(memory_space=pltpu.SMEM)


def anywhere():
    return pl.BlockSpec(memory_space=pl.ANY)


def pairs(offset, targets, field, columns):
    return pl.pallas_call(
        pair_kernel,
        out_shape=jax.ShapeDtypeStruct((MAX_ROWS // 128 + 2, 8, 128), F32),
        in_specs=[anywhere()] * 4,
        out_specs=in_vmem(),
        scratch_shapes=[
            pltpu.SMEM((1, 128), jnp.int32),
            pltpu.VMEM((TEAMS, 2, 128), F32),
            pltpu.VMEM((8, STARS_DEV), F32),
            pltpu.VMEM((STARS_DEV, 128), BF16),
            pltpu.SemaphoreType.DMA((4,)),
            pltpu.VMEM((8, MAX_ROWS + 256), F32),
            pltpu.VMEM((6, MAX_ROWS, 128), F32),
            pltpu.VMEM((MAX_ROWS, 128), F32),
            pltpu.VMEM((MAX_ROWS, 128), F32),
        ],
        compiler_params=pltpu.CompilerParams(vmem_limit_bytes=56 * 2**20),
        name="pairs",
    )(offset, targets, field, columns)


def body(position, velocity, accel, jerk, mass, elapsed, active_index):
    shape = jax.ShapeDtypeStruct
    message = pltpu.VMEM((TEAMS, 2, 128), F32)
    row = pltpu.VMEM((1, STARS_DEV), F32)
    triple = pltpu.VMEM((3, STARS_DEV), F32)
    dma = pltpu.SemaphoreType.DMA
    targets, offset, field, columns = pl.pallas_call(
        share_kernel,
        out_shape=(
            shape((TEAMS, 2, 128), F32),
            shape((1, 128), jnp.int32),
            shape((8, STARS_DEV), F32),
            shape((STARS_DEV, 128), BF16),
        ),
        in_specs=[in_smem()] + [anywhere()] * 6,
        out_specs=(in_vmem(), in_vmem(), anywhere(), anywhere()),
        scratch_shapes=[triple] * 4
        + [row] * 2
        + [
            pltpu.VMEM((8, STARS_DEV), F32),
            pltpu.VMEM((STARS_DEV, 128), BF16),
            pltpu.VMEM((2, 128), F32),
            message,
            dma((6,)),
            dma((2,)),
            dma,
            dma,
        ],
        compiler_params=pltpu.CompilerParams(collective_id=0, has_side_effects=True, vmem_limit_bytes=56 * 2**20),
        name="share",
    )(active_index, position, velocity, accel, jerk, mass[None, :], elapsed[None, :])
    sums = pairs(offset, targets, field, columns)
    ring = pl.pallas_call(
        total_kernel,
        out_shape=shape((REPS, 2, 128), F32),
        in_specs=[in_smem(), anywhere()],
        out_specs=in_vmem(),
        scratch_shapes=[
            pltpu.VMEM((MAX_ROWS // 128 + 2, 8, 128), F32),
            pltpu.VMEM((PLANE, Y_LOW, 2, 128), F32),
            pltpu.VMEM((PLANE, Y_LOW, 2, 128), F32),
            pltpu.VMEM((Y_LOW, 2, 128), F32),
            pltpu.VMEM((Y_LOW, REPS, 2, 128), F32),
            dma,
            dma,
            dma,
            dma,
            dma,
        ],
        compiler_params=pltpu.CompilerParams(collective_id=1, has_side_effects=True),
        name="totals",
    )(offset, sums)
    return pl.pallas_call(
        finish_kernel,
        out_shape=(shape((3, CAP), F32), shape((3, CAP), F32)),
        in_specs=[in_vmem(), in_vmem()],
        out_specs=(in_vmem(),) * 2,
        name="finish",
    )(ring, active_index[None, :])


def solution(mesh):
    in_specs = (
        P(None, "blk"),
        P(None, "blk"),
        P(None, "blk"),
        P(None, "blk"),
        P("blk"),
        P("blk"),
        P("blk"),
    )
    out_specs = (P(None, "blk"), P(None, "blk"))
    return jax.shard_map(body, mesh=mesh, in_specs=in_specs, out_specs=out_specs, check_vma=False)
```

```python
import functools

import jax
import jax.numpy as jnp
from jax import lax
from jax.experimental import pallas as pl
from jax.experimental.pallas import tpu as pltpu
from jax.sharding import PartitionSpec as P

SOFTENING = 0.001
MESH = pl.DeviceIdType.MESH
F32 = jnp.float32
BF16 = jnp.bfloat16
TEAMS = 64
REPS = 8
CAP = 256
SHARE = CAP // REPS
Z = 8
Y_LOW = 2
Y_HIGH = 4
PLANE = TEAMS // Y_LOW
STARS_DEV = 8192
MAX_ROWS = TEAMS * SHARE
GROUP = 16
EARLY = 96
UNROLL = 32


def iota(shape, dim):
    return lax.broadcasted_iota(jnp.int32, shape, dim)


def phase_of(team, rep):
    return lax.rem(rep + 3 * team, REPS)


def split3(x):
    a = x.astype(BF16)
    rest = x - a.astype(F32)
    b = rest.astype(BF16)
    c = (rest - b.astype(F32)).astype(BF16)
    return a, b, c


def fanned(rows, unit):
    sub = lax.rem(iota((8, 128), 0), 4)
    out = rows
    for k in range(1, 4):
        out = jnp.where(sub == k, pltpu.roll(rows, unit * k % 128, 1), out)
    return out


def signal_peers(barrier, axis, me, size):
    def one(step, carry):
        pl.semaphore_signal(
            barrier, inc=1, device_id={axis: lax.rem(me + step, size)}, device_id_type=MESH
        )
        return carry

    lax.fori_loop(1, size, one, 0)


def copy_all(pairs, sems):
    copies = [pltpu.make_async_copy(src, dst, sems.at[k]) for k, (src, dst) in enumerate(pairs)]
    for copy in copies:
        copy.start()
    return copies


def share_kernel(
    index_ref,
    pos_hbm,
    vel_hbm,
    acc_hbm,
    jrk_hbm,
    mass_hbm,
    elapsed_hbm,
    targets_out,
    offset_out,
    field_hbm,
    columns_hbm,
    pos,
    vel,
    acc,
    jrk,
    mass,
    elapsed,
    field,
    columns,
    own,
    recv,
    load_sem,
    store_sem,
    send_sem,
    recv_sem,
):
    team = lax.axis_index("blk")
    rep = lax.axis_index("rep")
    barrier = pltpu.get_barrier_semaphore()
    loads = copy_all(
        [(pos_hbm, pos), (vel_hbm, vel), (acc_hbm, acc), (jrk_hbm, jrk), (mass_hbm, mass), (elapsed_hbm, elapsed)],
        load_sem,
    )
    signal_peers(barrier, "blk", team, TEAMS)
    for copy in loads:
        copy.wait()

    h = elapsed[...]
    v, a, j = vel[...], acc[...], jrk[...]
    field[0:3, :] = pos[...] + h * (v + h * (0.5 * a + h / 6.0 * j))
    field[3:6, :] = v + h * (a + 0.5 * h * j)
    field[6:7, :] = mass[...]
    field[7:8, :] = jnp.ones((1, STARS_DEV), F32)
    stores = [pltpu.make_async_copy(field, field_hbm, store_sem.at[0])]
    stores[0].start()

    phase = phase_of(team, rep)
    lane = iota((8, 128), 1)
    sub = iota((8, 128), 0)
    picked = jnp.zeros((8, 128), F32)
    for group in range(2):
        slots = range(group * 16, group * 16 + 16)
        local = [index_ref[REPS * k + phase] - team * STARS_DEV for k in slots]

        def look(step, found):
            for k in range(4):
                at = pl.multiple_of(step * 512 + k * 128, 128)
                tile = field[:, pl.ds(at, 128)]
                number = lane + at
                found = tuple(jnp.where(number == want, tile, old) for want, old in zip(local, found))
            return found

        found = lax.fori_loop(0, STARS_DEV // 512, look, (jnp.zeros((8, 128), F32),) * 16)
        for k, one in zip(slots, found):
            picked = jnp.where(lane == k, jnp.sum(one, axis=1, keepdims=True), picked)
    picked = jnp.where(sub == 6, pltpu.roll(picked, 7, 0), picked)
    spread = fanned(jnp.where(lane < SHARE, picked, 0.0), 32)
    spread = spread + pltpu.roll(spread, 6, 0)
    spread = spread + pltpu.roll(spread, 7, 0)
    own[0:1, :] = spread[0:1, :]
    own[1:2, :] = spread[4:5, :]
    recv[team] = jnp.concatenate([spread[0:1, :], spread[4:5, :]], 0)

    pl.semaphore_wait(barrier, TEAMS - 1)

    def send(step, carry):
        pltpu.make_async_remote_copy(
            src_ref=own,
            dst_ref=recv.at[team],
            send_sem=send_sem,
            recv_sem=recv_sem,
            device_id={"blk": lax.rem(team + step, TEAMS)},
            device_id_type=MESH,
        ).start()
        return carry

    lax.fori_loop(1, TEAMS, send, 0)

    def source_tile(step, carry):
        for k in range(4):
            at = pl.multiple_of(step * 512 + k * 128, 128)
            rows = field[:, pl.ds(at, 128)]
            weighted = jnp.where(sub < 6, rows * rows[6:7, :], rows)
            a, b, c = (part.astype(F32) for part in split3(weighted))
            stack = jnp.concatenate([a, b, c, jnp.zeros((104, 128), F32)], 0)
            columns[pl.ds(at, 128), :] = jnp.transpose(stack).astype(BF16)
        return carry

    lax.fori_loop(0, STARS_DEV // 512, source_tile, 0)
    stores.append(pltpu.make_async_copy(columns, columns_hbm, store_sem.at[1]))
    stores[1].start()
    pltpu.make_async_copy(recv.at[pl.ds(0, TEAMS - 1)], recv.at[pl.ds(0, TEAMS - 1)], recv_sem).wait()
    pltpu.make_async_copy(recv.at[pl.ds(0, TEAMS - 1)], recv.at[pl.ds(0, TEAMS - 1)], send_sem).wait()
    got = recv[...]
    targets_out[...] = got
    flag_lanes = iota((TEAMS, 128), 1)
    flags = jnp.where((flag_lanes >= 64) & (flag_lanes < 96), got[:, 1, :], 0.0)
    counts = jnp.sum(flags, axis=1, keepdims=True)
    before = jnp.where(iota((TEAMS, 128), 0) < flag_lanes, counts, 0.0)
    offset_out[...] = jnp.sum(before, axis=0, keepdims=True).astype(jnp.int32)
    for copy in stores:
        copy.wait()


def spread_targets(rows, tb, at):
    for k in range(6):
        tb[k, pl.ds(at, 128), :] = jnp.transpose(jnp.broadcast_to(rows[k : k + 1, :], (128, 128)))


def folded_sums(rows, sum_s, sum_t, at):
    sub = iota((8, 128), 0)

    def folded(ref):
        cols = jnp.transpose(ref[pl.ds(at, 128), :])
        part = cols[0:8] + cols[8:16] + cols[16:24]
        return part - rows * part[6:7, :]

    g_s, g_t = folded(sum_s), folded(sum_t)
    g_t = pltpu.roll(g_t, 3, 0)
    out = jnp.where((sub >= 3) & (sub < 6), g_s - 3.0 * g_t, g_s)
    return jnp.where(sub < 6, out, 0.0)


def block_adder(field, columns, tb, sum_s, sum_t):
    chunks = STARS_DEV // 512

    def stage(chunk, register):
        for m in range(2):
            cols = pl.ds(pl.multiple_of(chunk * 512 + m * 256, 256), 256)
            rhs = jnp.concatenate([columns[cols, :], jnp.zeros((256, 128), BF16)], 1)
            pltpu.matmul_push_rhs(rhs, register, m)

    def add_chunk(at, chunk, register, acc_s, acc_t):
        for g in range(len(acc_s[0])):
            rows = pl.ds(at + g * GROUP, GROUP)
            for m in range(2):
                parts = [[], [], [], []]
                for half in range(2):
                    cols = pl.ds(pl.multiple_of(chunk * 512 + m * 256 + half * 128, 128), 128)
                    d = [field[c : c + 1, cols] - tb[c, rows, :] for c in range(3)]
                    w = [field[c + 3 : c + 4, cols] - tb[c + 3, rows, :] for c in range(3)]
                    r2 = d[0] * d[0] + d[1] * d[1] + d[2] * d[2] + SOFTENING
                    q = lax.rsqrt(r2)
                    u = d[0] * w[0] + d[1] * w[1] + d[2] * w[2]
                    q2 = q * q
                    s = q * q2
                    t = (u * q2) * s
                    s_hi, t_hi = s.astype(BF16), t.astype(BF16)
                    parts[0].append(s_hi)
                    parts[1].append(s - s_hi.astype(F32))
                    parts[2].append(t_hi)
                    parts[3].append(t - t_hi.astype(F32))
                parts = [jnp.concatenate(pair, 1) for pair in parts]
                first = register if g == 0 else None
                pltpu.matmul_acc_lhs(acc_s[m][g], parts[0], load_staged_rhs=first)
                pltpu.matmul_acc_lhs(acc_s[m][g], parts[1])
                pltpu.matmul_acc_lhs(acc_t[m][g], parts[2])
                pltpu.matmul_acc_lhs(acc_t[m][g], parts[3])

    def add_blocks(size, base, count, unroll):
        groups = size // GROUP

        def scoped(*accs):
            acc_s = [accs[m * groups : (m + 1) * groups] for m in range(2)]
            acc_t = [accs[(2 + m) * groups : (3 + m) * groups] for m in range(2)]

            def block(number, carry):
                at = pl.multiple_of(base + number * size, 32)
                stage(0, 0)

                def some_chunks(step, inner):
                    for k in range(unroll):
                        chunk = step * unroll + k
                        stage(jnp.minimum(chunk + 1, chunks - 1), 1 - k % 2)
                        add_chunk(at, chunk, k % 2, acc_s, acc_t)
                    return inner

                lax.fori_loop(0, chunks // unroll, some_chunks, 0)
                for g in range(groups):
                    rows = pl.ds(at + g * GROUP, GROUP)
                    sum_s[rows, :] = pltpu.matmul_pop(acc_s[0][g])[:, :128] + pltpu.matmul_pop(acc_s[1][g])[:, :128]
                    sum_t[rows, :] = pltpu.matmul_pop(acc_t[0][g])[:, :128] + pltpu.matmul_pop(acc_t[1][g])[:, :128]
                for m in range(2):
                    pltpu.matmul_acc_lhs(acc_s[m][0], jnp.zeros((GROUP, 256), BF16), load_staged_rhs=0)
                    pltpu.matmul_pop(acc_s[m][0])
                return carry

            lax.fori_loop(0, count, block, 0)

        sets = []
        for m in (0, 1, 0, 1):
            sets += [pltpu.ACC(m)((GROUP, 256), F32)] * groups
        pl.run_scoped(scoped, *sets)

    return add_blocks


def pair_kernel(
    offset_hbm, targets_hbm, field_hbm, columns_hbm, sums_out, first_out,
    offset, targets, field, columns, load_sem, comp, tb, sum_s, sum_t,
):
    loads = copy_all(
        [(offset_hbm, offset), (targets_hbm, targets), (field_hbm, field), (columns_hbm, columns)], load_sem
    )
    lane = iota((8, 128), 1)
    sub = iota((8, 128), 0)
    loads[0].wait()
    loads[1].wait()
    total = offset[0, TEAMS]
    tiles = lax.div(total + 127, 128)

    def clear(tile, carry):
        comp[:, pl.ds(pl.multiple_of(tile * 128, 128), 128)] = jnp.zeros((8, 128), F32)
        return carry

    lax.fori_loop(0, tiles + 2, clear, 0)

    def compact(step, carry):
        ready = []
        for k in range(UNROLL):
            team = step * UNROLL + k
            start = offset[0, team]
            count = offset[0, team + 1] - start
            message = targets[team]
            rows = jnp.where(sub < 4, message[0:1, :], message[1:2, :])
            rows = jnp.where(lane < count, fanned(rows, 96), 0.0)
            shift = lax.rem(start, 128)
            ready.append((pl.multiple_of(lax.div(start, 128) * 128, 128), shift, pltpu.roll(rows, shift, 1)))
        for first, shift, rows in ready:
            comp[:, pl.ds(first, 128)] += jnp.where(lane >= shift, rows, 0.0)
            comp[:, pl.ds(first + 128, 128)] += jnp.where(lane < shift, rows, 0.0)
        return carry

    lax.fori_loop(0, TEAMS // UNROLL, compact, 0)

    def target_tile(tile, carry):
        at = pl.multiple_of(tile * 128, 128)
        spread_targets(comp[:, pl.ds(at, 128)], tb, at)
        return carry

    lax.fori_loop(0, tiles, target_tile, 0)
    first_out[...] = comp[:, 0:128]
    loads[2].wait()
    loads[3].wait()

    add_blocks = block_adder(field, columns, tb, sum_s, sum_t)
    left = jnp.maximum(total - EARLY, 0)
    whole = lax.div(left, 96)
    rest = left - whole * 96
    base = EARLY + whole * 96
    one = jnp.int32(1)
    none = jnp.int32(0)
    add_blocks(96, EARLY, whole + jnp.where(rest > 64, one, none), 4)
    add_blocks(64, base, jnp.where((rest > 32) & (rest <= 64), one, none), 4)
    add_blocks(32, base, jnp.where((rest > 0) & (rest <= 32), one, none), 4)

    def result_tile(tile, carry):
        at = pl.multiple_of(tile * 128, 128)
        sums_out[tile] = folded_sums(comp[:, pl.ds(at, 128)], sum_s, sum_t, at)
        return carry

    lax.fori_loop(0, tiles, result_tile, 0)


def total_kernel(
    offset, first_rows, sums_hbm, field_hbm, columns_hbm, ring_out,
    sums, field, columns, tb, sum_s, sum_t, partial, recv, mine, column, half,
    load_sem, send_sem, recv_sem, send_sem2, recv_sem2, send_sem3, recv_sem3,
):
    team = lax.axis_index("blk")
    rep = lax.axis_index("rep")
    depth = lax.rem(team, Z)
    low = lax.rem(lax.div(team, Z), Y_LOW)
    wide = lax.div(team, Z * Y_LOW)
    core = lax.rem(rep, 2)
    high = lax.div(rep, 2)
    place = wide * Z + depth
    stack = low * Y_HIGH + high

    def team_of(place, low):
        return (lax.div(place, Z) * Y_LOW + low) * Z + lax.rem(place, Z)

    def plane_peer(step):
        return lax.rem(place + step, PLANE)

    def stack_peer(step):
        other = lax.rem(stack + step, Y_LOW * Y_HIGH)
        return lax.div(other, Y_HIGH), lax.rem(other, Y_HIGH)

    barrier = pltpu.get_barrier_semaphore()
    loads = copy_all([(field_hbm, field), (columns_hbm, columns), (sums_hbm, sums)], load_sem)

    def greet_plane(step, carry):
        pl.semaphore_signal(
            barrier, inc=1, device_id={"blk": team_of(plane_peer(step), low), "rep": rep}, device_id_type=MESH
        )
        return carry

    def greet_stack(step, carry):
        peer_low, peer_high = stack_peer(step)
        pl.semaphore_signal(
            barrier,
            inc=1,
            device_id={"blk": team_of(place, peer_low), "rep": peer_high * 2 + core},
            device_id_type=MESH,
        )
        return carry

    lax.fori_loop(1, PLANE, greet_plane, 0)
    lax.fori_loop(1, Y_LOW * Y_HIGH, greet_stack, 0)
    pl.semaphore_signal(barrier, inc=1, device_id={"blk": team, "rep": high * 2 + 1 - core}, device_id_type=MESH)

    spread_targets(first_rows[...], tb, 0)
    for copy in loads:
        copy.wait()
    block_adder(field, columns, tb, sum_s, sum_t)(EARLY, 0, 1, 4)
    lane = iota((8, 128), 1)
    sums[0] = jnp.where(lane < EARLY, folded_sums(first_rows[...], sum_s, sum_t, 0), sums[0])

    for k in range(TEAMS):
        start = offset[0, k]
        count = offset[0, k + 1] - start
        first = lax.div(start, 128)
        shift = lax.rem(start, 128)
        both = jnp.where(lane >= shift, sums[first], sums[first + 1])
        rows = pltpu.roll(both, lax.rem(128 - shift, 128), 1)
        rows = fanned(jnp.where(lane < count, rows, 0.0), 32)
        rows = rows + pltpu.roll(rows, 6, 0)
        rows = rows + pltpu.roll(rows, 7, 0)
        at = k // (Z * Y_LOW) * Z + k % Z
        partial[at, k // Z % Y_LOW, 0:1, :] = rows[0:1, :]
        partial[at, k // Z % Y_LOW, 1:2, :] = rows[4:5, :]

    recv[place] = partial[place]
    pl.semaphore_wait(barrier, PLANE + Y_LOW * Y_HIGH - 1)

    def send(step, carry):
        peer = plane_peer(step)
        pltpu.make_async_remote_copy(
            src_ref=partial.at[peer],
            dst_ref=recv.at[place],
            send_sem=send_sem,
            recv_sem=recv_sem,
            device_id={"blk": team_of(peer, low), "rep": rep},
            device_id_type=MESH,
        ).start()
        return carry

    lax.fori_loop(1, PLANE, send, 0)
    pltpu.make_async_copy(recv.at[pl.ds(0, PLANE - 1)], recv.at[pl.ds(0, PLANE - 1)], recv_sem).wait()
    summed = jnp.sum(recv[...], axis=0)
    mine[...] = summed
    column[low, high] = mine[low]

    def pass_on(step, carry):
        peer_low, peer_high = stack_peer(step)
        pltpu.make_async_remote_copy(
            src_ref=mine.at[peer_low],
            dst_ref=column.at[low, high],
            send_sem=send_sem2,
            recv_sem=recv_sem2,
            device_id={"blk": team_of(place, peer_low), "rep": peer_high * 2 + core},
            device_id_type=MESH,
        ).start()
        return carry

    lax.fori_loop(1, Y_LOW * Y_HIGH, pass_on, 0)
    pltpu.make_async_copy(recv.at[pl.ds(0, PLANE - 1)], recv.at[pl.ds(0, PLANE - 1)], send_sem).wait()
    flat = partial.at[pl.ds(0, Y_LOW * Y_HIGH - 1), 0]
    pltpu.make_async_copy(flat, flat, recv_sem2).wait()
    pltpu.make_async_copy(flat, flat, send_sem2).wait()
    half[core] = column[0] + column[1]
    swap = pltpu.make_async_remote_copy(
        src_ref=half.at[core],
        dst_ref=half.at[core],
        send_sem=send_sem3,
        recv_sem=recv_sem3,
        device_id={"blk": team, "rep": high * 2 + 1 - core},
        device_id_type=MESH,
    )
    swap.start()
    swap.wait()
    for k in range(REPS):
        ring_out[phase_of(team, k)] = half[k % 2, k // 2]


def finish_kernel(ring, live, force, new_jerk):
    source = iota((CAP, CAP), 0)
    slot = iota((CAP, CAP), 1)
    place = jnp.where(slot == lax.rem(source, SHARE) * REPS + lax.div(source, SHARE), 1.0, 0.0).astype(BF16)
    lane = iota((8, 128), 1)
    sub = iota((8, 128), 0)
    halves = []
    for half in range(2):
        tile = jnp.zeros((8, 128), F32)
        for k in range(4):
            message = ring[half * 4 + k]
            rows = jnp.where(sub < 4, message[0:1, :], message[1:2, :])
            rows = fanned(rows, 96)
            rows = rows if k == 0 else pltpu.roll(rows, 32 * k, 1)
            tile = jnp.where(lane // 32 == k, rows, tile)
        halves.append(tile)
    x = jnp.concatenate(halves, 1)
    a, b, c = (part.astype(F32) for part in split3(x))
    stack = jnp.concatenate([a, b, c, jnp.zeros((8, CAP), F32)], 0).astype(BF16)
    moved = jnp.dot(stack, place, preferred_element_type=F32)
    sums = moved[0:8] + moved[8:16] + moved[16:24]
    scaled = jnp.where(live[...] >= 0, sums / (STARS_DEV * TEAMS), 0.0)
    force[...] = scaled[0:3]
    new_jerk[...] = scaled[3:6]


def in_vmem():
    return pl.BlockSpec(memory_space=pltpu.VMEM)


def in_smem():
    return pl.BlockSpec(memory_space=pltpu.SMEM)


def anywhere():
    return pl.BlockSpec(memory_space=pl.ANY)


def pairs(offset, targets, field, columns):
    return pl.pallas_call(
        pair_kernel,
        out_shape=(
            jax.ShapeDtypeStruct((MAX_ROWS // 128 + 2, 8, 128), F32),
            jax.ShapeDtypeStruct((8, 128), F32),
        ),
        in_specs=[anywhere()] * 4,
        out_specs=(in_vmem(),) * 2,
        scratch_shapes=[
            pltpu.SMEM((1, 128), jnp.int32),
            pltpu.VMEM((TEAMS, 2, 128), F32),
            pltpu.VMEM((8, STARS_DEV), F32),
            pltpu.VMEM((STARS_DEV, 128), BF16),
            pltpu.SemaphoreType.DMA((4,)),
            pltpu.VMEM((8, MAX_ROWS + 256), F32),
            pltpu.VMEM((6, MAX_ROWS, 128), F32),
            pltpu.VMEM((MAX_ROWS, 128), F32),
            pltpu.VMEM((MAX_ROWS, 128), F32),
        ],
        compiler_params=pltpu.CompilerParams(vmem_limit_bytes=56 * 2**20),
        name="pairs",
    )(offset, targets, field, columns)


def body(position, velocity, accel, jerk, mass, elapsed, active_index):
    shape = jax.ShapeDtypeStruct
    message = pltpu.VMEM((TEAMS, 2, 128), F32)
    row = pltpu.VMEM((1, STARS_DEV), F32)
    triple = pltpu.VMEM((3, STARS_DEV), F32)
    dma = pltpu.SemaphoreType.DMA
    targets, offset, field, columns = pl.pallas_call(
        share_kernel,
        out_shape=(
            shape((TEAMS, 2, 128), F32),
            shape((1, 128), jnp.int32),
            shape((8, STARS_DEV), F32),
            shape((STARS_DEV, 128), BF16),
        ),
        in_specs=[in_smem()] + [anywhere()] * 6,
        out_specs=(in_vmem(), in_vmem(), anywhere(), anywhere()),
        scratch_shapes=[triple] * 4
        + [row] * 2
        + [
            pltpu.VMEM((8, STARS_DEV), F32),
            pltpu.VMEM((STARS_DEV, 128), BF16),
            pltpu.VMEM((2, 128), F32),
            message,
            dma((6,)),
            dma((2,)),
            dma,
            dma,
        ],
        compiler_params=pltpu.CompilerParams(collective_id=0, has_side_effects=True, vmem_limit_bytes=56 * 2**20),
        name="share",
    )(active_index, position, velocity, accel, jerk, mass[None, :], elapsed[None, :])
    sums, first_rows = pairs(offset, targets, field, columns)
    ring = pl.pallas_call(
        total_kernel,
        out_shape=shape((REPS, 2, 128), F32),
        in_specs=[in_smem(), in_vmem()] + [anywhere()] * 3,
        out_specs=in_vmem(),
        scratch_shapes=[
            pltpu.VMEM((MAX_ROWS // 128 + 2, 8, 128), F32),
            pltpu.VMEM((8, STARS_DEV), F32),
            pltpu.VMEM((STARS_DEV, 128), BF16),
            pltpu.VMEM((6, 128, 128), F32),
            pltpu.VMEM((128, 128), F32),
            pltpu.VMEM((128, 128), F32),
            pltpu.VMEM((PLANE, Y_LOW, 2, 128), F32),
            pltpu.VMEM((PLANE, Y_LOW, 2, 128), F32),
            pltpu.VMEM((Y_LOW, 2, 128), F32),
            pltpu.VMEM((Y_LOW, Y_HIGH, 2, 128), F32),
            pltpu.VMEM((2, Y_HIGH, 2, 128), F32),
            dma((3,)),
        ]
        + [dma] * 6,
        compiler_params=pltpu.CompilerParams(collective_id=1, has_side_effects=True, vmem_limit_bytes=56 * 2**20),
        name="totals",
    )(offset, first_rows, sums, field, columns)
    return pl.pallas_call(
        finish_kernel,
        out_shape=(shape((3, CAP), F32), shape((3, CAP), F32)),
        in_specs=[in_vmem(), in_vmem()],
        out_specs=(in_vmem(),) * 2,
        name="finish",
    )(ring, active_index[None, :])


def solution(mesh):
    in_specs = (
        P(None, "blk"),
        P(None, "blk"),
        P(None, "blk"),
        P(None, "blk"),
        P("blk"),
        P("blk"),
        P("blk"),
    )
    out_specs = (P(None, "blk"), P(None, "blk"))
    return jax.shard_map(body, mesh=mesh, in_specs=in_specs, out_specs=out_specs, check_vma=False)
```

```python
import functools

import jax
import jax.numpy as jnp
from jax import lax
from jax.experimental import pallas as pl
from jax.experimental.pallas import tpu as pltpu
from jax.sharding import PartitionSpec as P

SOFTENING = 0.001
MESH = pl.DeviceIdType.MESH
F32 = jnp.float32
BF16 = jnp.bfloat16
TEAMS = 64
REPS = 8
CAP = 256
SHARE = CAP // REPS
Z = 8
Y_LOW = 2
PLANE = TEAMS // Y_LOW
STARS_DEV = 8192
MAX_ROWS = TEAMS * SHARE
GROUP = 16
EARLY = 96
UNROLL = 32


def iota(shape, dim):
    return lax.broadcasted_iota(jnp.int32, shape, dim)


def phase_of(team, rep):
    return lax.rem(rep + 3 * team, REPS)


def split3(x):
    a = x.astype(BF16)
    rest = x - a.astype(F32)
    b = rest.astype(BF16)
    c = (rest - b.astype(F32)).astype(BF16)
    return a, b, c


def fanned(rows, unit):
    sub = lax.rem(iota((8, 128), 0), 4)
    out = rows
    for k in range(1, 4):
        out = jnp.where(sub == k, pltpu.roll(rows, unit * k % 128, 1), out)
    return out


def for_peers(size, far, act):
    def down(k, carry):
        act(far - k)
        return carry

    def rest(k, carry):
        act(size - 1 - k)
        return carry

    lax.fori_loop(0, far, down, 0)
    lax.fori_loop(0, size - 1 - far, rest, 0)


def copy_all(pairs, sems):
    copies = [pltpu.make_async_copy(src, dst, sems.at[k]) for k, (src, dst) in enumerate(pairs)]
    for copy in copies:
        copy.start()
    return copies


def share_kernel(
    index_ref,
    pos_hbm,
    vel_hbm,
    acc_hbm,
    jrk_hbm,
    mass_hbm,
    elapsed_hbm,
    targets_out,
    offset_out,
    field_hbm,
    columns_hbm,
    pos,
    vel,
    acc,
    jrk,
    mass,
    elapsed,
    field,
    columns,
    own,
    recv,
    load_sem,
    store_sem,
    send_sem,
    recv_sem,
):
    team = lax.axis_index("blk")
    rep = lax.axis_index("rep")
    barrier = pltpu.get_barrier_semaphore()
    loads = copy_all(
        [(pos_hbm, pos), (vel_hbm, vel), (acc_hbm, acc), (jrk_hbm, jrk), (mass_hbm, mass), (elapsed_hbm, elapsed)],
        load_sem,
    )

    def greet(offset):
        peer = lax.rem(team + offset, TEAMS)
        pl.semaphore_signal(barrier, inc=1, device_id={"blk": peer}, device_id_type=MESH)

    for_peers(TEAMS, 47, greet)
    for copy in loads:
        copy.wait()

    h = elapsed[...]
    v, a, j = vel[...], acc[...], jrk[...]
    field[0:3, :] = pos[...] + h * (v + h * (0.5 * a + h / 6.0 * j))
    field[3:6, :] = v + h * (a + 0.5 * h * j)
    field[6:7, :] = mass[...]
    field[7:8, :] = jnp.ones((1, STARS_DEV), F32)
    stores = [pltpu.make_async_copy(field, field_hbm, store_sem.at[0])]
    stores[0].start()

    phase = phase_of(team, rep)
    lane = iota((8, 128), 1)
    sub = iota((8, 128), 0)
    picked = jnp.zeros((8, 128), F32)
    for group in range(2):
        slots = range(group * 16, group * 16 + 16)
        local = [index_ref[REPS * k + phase] - team * STARS_DEV for k in slots]

        def look(step, found):
            for k in range(4):
                at = pl.multiple_of(step * 512 + k * 128, 128)
                tile = field[:, pl.ds(at, 128)]
                number = lane + at
                found = tuple(jnp.where(number == want, tile, old) for want, old in zip(local, found))
            return found

        found = lax.fori_loop(0, STARS_DEV // 512, look, (jnp.zeros((8, 128), F32),) * 16)
        for k, one in zip(slots, found):
            picked = jnp.where(lane == k, jnp.sum(one, axis=1, keepdims=True), picked)
    picked = jnp.where(sub == 6, pltpu.roll(picked, 7, 0), picked)
    spread = fanned(jnp.where(lane < SHARE, picked, 0.0), 32)
    spread = spread + pltpu.roll(spread, 6, 0)
    spread = spread + pltpu.roll(spread, 7, 0)
    own[0:1, :] = spread[0:1, :]
    own[1:2, :] = spread[4:5, :]
    recv[team] = jnp.concatenate([spread[0:1, :], spread[4:5, :]], 0)

    pl.semaphore_wait(barrier, TEAMS - 1)

    def send(offset):
        pltpu.make_async_remote_copy(
            src_ref=own,
            dst_ref=recv.at[team],
            send_sem=send_sem,
            recv_sem=recv_sem,
            device_id={"blk": lax.rem(team + offset, TEAMS)},
            device_id_type=MESH,
        ).start()

    for_peers(TEAMS, 47, send)

    def source_tile(step, carry):
        for k in range(4):
            at = pl.multiple_of(step * 512 + k * 128, 128)
            rows = field[:, pl.ds(at, 128)]
            weighted = jnp.where(sub < 6, rows * rows[6:7, :], rows)
            a, b, c = (part.astype(F32) for part in split3(weighted))
            stack = jnp.concatenate([a, b, c, jnp.zeros((104, 128), F32)], 0)
            columns[pl.ds(at, 128), :] = jnp.transpose(stack).astype(BF16)
        return carry

    lax.fori_loop(0, STARS_DEV // 512, source_tile, 0)
    stores.append(pltpu.make_async_copy(columns, columns_hbm, store_sem.at[1]))
    stores[1].start()
    pltpu.make_async_copy(recv.at[pl.ds(0, TEAMS - 1)], recv.at[pl.ds(0, TEAMS - 1)], recv_sem).wait()
    pltpu.make_async_copy(recv.at[pl.ds(0, TEAMS - 1)], recv.at[pl.ds(0, TEAMS - 1)], send_sem).wait()
    got = recv[...]
    targets_out[...] = got
    flag_lanes = iota((TEAMS, 128), 1)
    flags = jnp.where((flag_lanes >= 64) & (flag_lanes < 96), got[:, 1, :], 0.0)
    counts = jnp.sum(flags, axis=1, keepdims=True)
    before = jnp.where(iota((TEAMS, 128), 0) < flag_lanes, counts, 0.0)
    offset_out[...] = jnp.sum(before, axis=0, keepdims=True).astype(jnp.int32)
    for copy in stores:
        copy.wait()


def spread_targets(rows, tb, at):
    for k in range(6):
        tb[k, pl.ds(at, 128), :] = jnp.transpose(jnp.broadcast_to(rows[k : k + 1, :], (128, 128)))


def folded_sums(rows, sum_s, sum_t, at):
    sub = iota((8, 128), 0)

    def folded(ref):
        cols = jnp.transpose(ref[pl.ds(at, 128), :])
        part = cols[0:8] + cols[8:16] + cols[16:24]
        return part - rows * part[6:7, :]

    g_s, g_t = folded(sum_s), folded(sum_t)
    g_t = pltpu.roll(g_t, 3, 0)
    out = jnp.where((sub >= 3) & (sub < 6), g_s - 3.0 * g_t, g_s)
    return jnp.where(sub < 6, out, 0.0)


def block_adder(field, columns, tb, sum_s, sum_t):
    chunks = STARS_DEV // 512

    def stage(chunk, register):
        for m in range(2):
            cols = pl.ds(pl.multiple_of(chunk * 512 + m * 256, 256), 256)
            rhs = jnp.concatenate([columns[cols, :], jnp.zeros((256, 128), BF16)], 1)
            pltpu.matmul_push_rhs(rhs, register, m)

    def add_chunk(at, chunk, register, acc_s, acc_t):
        for g in range(len(acc_s[0])):
            rows = pl.ds(at + g * GROUP, GROUP)
            for m in range(2):
                parts = [[], [], [], []]
                for half in range(2):
                    cols = pl.ds(pl.multiple_of(chunk * 512 + m * 256 + half * 128, 128), 128)
                    d = [field[c : c + 1, cols] - tb[c, rows, :] for c in range(3)]
                    w = [field[c + 3 : c + 4, cols] - tb[c + 3, rows, :] for c in range(3)]
                    r2 = d[0] * d[0] + d[1] * d[1] + d[2] * d[2] + SOFTENING
                    q = lax.rsqrt(r2)
                    u = d[0] * w[0] + d[1] * w[1] + d[2] * w[2]
                    q2 = q * q
                    s = q * q2
                    t = (u * q2) * s
                    s_hi, t_hi = s.astype(BF16), t.astype(BF16)
                    parts[0].append(s_hi)
                    parts[1].append(s - s_hi.astype(F32))
                    parts[2].append(t_hi)
                    parts[3].append(t - t_hi.astype(F32))
                parts = [jnp.concatenate(pair, 1) for pair in parts]
                first = register if g == 0 else None
                pltpu.matmul_acc_lhs(acc_s[m][g], parts[0], load_staged_rhs=first)
                pltpu.matmul_acc_lhs(acc_s[m][g], parts[1])
                pltpu.matmul_acc_lhs(acc_t[m][g], parts[2])
                pltpu.matmul_acc_lhs(acc_t[m][g], parts[3])

    def add_blocks(size, base, count, unroll, before=None):
        groups = size // GROUP

        def scoped(*accs):
            acc_s = [accs[m * groups : (m + 1) * groups] for m in range(2)]
            acc_t = [accs[(2 + m) * groups : (3 + m) * groups] for m in range(2)]

            def block(number, carry):
                at = pl.multiple_of(base + number * size, 32)
                stage(0, 0)

                def some_chunks(step, inner):
                    if before is not None:
                        before(step)
                    for k in range(unroll):
                        chunk = step * unroll + k
                        stage(jnp.minimum(chunk + 1, chunks - 1), 1 - k % 2)
                        add_chunk(at, chunk, k % 2, acc_s, acc_t)
                    return inner

                lax.fori_loop(0, chunks // unroll, some_chunks, 0)
                for g in range(groups):
                    rows = pl.ds(at + g * GROUP, GROUP)
                    sum_s[rows, :] = pltpu.matmul_pop(acc_s[0][g])[:, :128] + pltpu.matmul_pop(acc_s[1][g])[:, :128]
                    sum_t[rows, :] = pltpu.matmul_pop(acc_t[0][g])[:, :128] + pltpu.matmul_pop(acc_t[1][g])[:, :128]
                for m in range(2):
                    pltpu.matmul_acc_lhs(acc_s[m][0], jnp.zeros((GROUP, 256), BF16), load_staged_rhs=0)
                    pltpu.matmul_pop(acc_s[m][0])
                return carry

            lax.fori_loop(0, count, block, 0)

        sets = []
        for m in (0, 1, 0, 1):
            sets += [pltpu.ACC(m)((GROUP, 256), F32)] * groups
        pl.run_scoped(scoped, *sets)

    return add_blocks


def pair_kernel(
    offset_hbm, targets_hbm, field_hbm, columns_hbm, sums_out, first_out,
    offset, targets, field, columns, load_sem, comp, tb, sum_s, sum_t,
):
    loads = copy_all(
        [(offset_hbm, offset), (targets_hbm, targets), (field_hbm, field), (columns_hbm, columns)], load_sem
    )
    lane = iota((8, 128), 1)
    sub = iota((8, 128), 0)
    loads[0].wait()
    loads[1].wait()
    total = offset[0, TEAMS]
    tiles = lax.div(total + 127, 128)

    def clear(tile, carry):
        comp[:, pl.ds(pl.multiple_of(tile * 128, 128), 128)] = jnp.zeros((8, 128), F32)
        return carry

    lax.fori_loop(0, tiles + 2, clear, 0)

    def compact(step, carry):
        ready = []
        for k in range(UNROLL):
            team = step * UNROLL + k
            start = offset[0, team]
            count = offset[0, team + 1] - start
            message = targets[team]
            rows = jnp.where(sub < 4, message[0:1, :], message[1:2, :])
            rows = jnp.where(lane < count, fanned(rows, 96), 0.0)
            shift = lax.rem(start, 128)
            ready.append((pl.multiple_of(lax.div(start, 128) * 128, 128), shift, pltpu.roll(rows, shift, 1)))
        for first, shift, rows in ready:
            comp[:, pl.ds(first, 128)] += jnp.where(lane >= shift, rows, 0.0)
            comp[:, pl.ds(first + 128, 128)] += jnp.where(lane < shift, rows, 0.0)
        return carry

    lax.fori_loop(0, TEAMS // UNROLL, compact, 0)

    def target_tile(tile, carry):
        at = pl.multiple_of(tile * 128, 128)
        spread_targets(comp[:, pl.ds(at, 128)], tb, at)
        return carry

    lax.fori_loop(0, tiles, target_tile, 0)
    first_out[...] = comp[:, 0:128]
    loads[2].wait()
    loads[3].wait()

    add_blocks = block_adder(field, columns, tb, sum_s, sum_t)
    left = jnp.maximum(total - EARLY, 0)
    whole = lax.div(left, 96)
    rest = left - whole * 96
    base = EARLY + whole * 96
    one = jnp.int32(1)
    none = jnp.int32(0)
    add_blocks(96, EARLY, whole + jnp.where(rest > 64, one, none), 4)
    add_blocks(64, base, jnp.where((rest > 32) & (rest <= 64), one, none), 4)
    add_blocks(32, base, jnp.where((rest > 0) & (rest <= 32), one, none), 4)

    def result_tile(tile, carry):
        at = pl.multiple_of(tile * 128, 128)
        sums_out[tile] = folded_sums(comp[:, pl.ds(at, 128)], sum_s, sum_t, at)
        return carry

    lax.fori_loop(0, tiles, result_tile, 0)


def total_kernel(
    offset, first_rows, sums_hbm, field_hbm, columns_hbm, ring_out,
    sums, field, columns, tb, sum_s, sum_t, partial, recv, mine, column,
    load_sem, send_sem, recv_sem, send_sem2, recv_sem2,
):
    team = lax.axis_index("blk")
    rep = lax.axis_index("rep")
    depth = lax.rem(team, Z)
    low = lax.rem(lax.div(team, Z), Y_LOW)
    wide = lax.div(team, Z * Y_LOW)
    place = wide * Z + depth
    stack = low * REPS + rep

    def team_of(place, low):
        return (lax.div(place, Z) * Y_LOW + low) * Z + lax.rem(place, Z)

    def plane_peer(step):
        return lax.rem(place + step, PLANE)

    def column_peer(step):
        other = lax.rem(stack + step, Y_LOW * REPS)
        return lax.div(other, REPS), lax.rem(other, REPS)

    barrier = pltpu.get_barrier_semaphore()

    def quarter(n):
        return columns_hbm.at[pl.ds(n * 2048, 2048)], columns.at[pl.ds(n * 2048, 2048)]

    loads = copy_all([(field_hbm, field)] + [quarter(n) for n in range(4)] + [(sums_hbm, sums)], load_sem)

    def greet_plane(offset):
        peer = team_of(plane_peer(offset), low)
        pl.semaphore_signal(barrier, inc=1, device_id={"blk": peer, "rep": rep}, device_id_type=MESH)

    def greet_column(step, carry):
        peer_low, peer_rep = column_peer(step)
        pl.semaphore_signal(
            barrier, inc=1, device_id={"blk": team_of(place, peer_low), "rep": peer_rep}, device_id_type=MESH
        )
        return carry

    for_peers(PLANE, 23, greet_plane)
    lax.fori_loop(1, Y_LOW * REPS, greet_column, 0)

    spread_targets(first_rows[...], tb, 0)
    loads[0].wait()
    loads[1].wait()

    def await_quarter(step):
        @pl.when(step < 3)
        def _():
            ahead = pl.multiple_of(step * 2048 + 2048, 2048)
            pltpu.make_async_copy(
                columns_hbm.at[pl.ds(ahead, 2048)], columns.at[pl.ds(ahead, 2048)], load_sem.at[step + 2]
            ).wait()

    block_adder(field, columns, tb, sum_s, sum_t)(EARLY, 0, 1, 4, await_quarter)
    loads[5].wait()
    lane = iota((8, 128), 1)
    sums[0] = jnp.where(lane < EARLY, folded_sums(first_rows[...], sum_s, sum_t, 0), sums[0])

    for k in range(TEAMS):
        start = offset[0, k]
        count = offset[0, k + 1] - start
        first = lax.div(start, 128)
        shift = lax.rem(start, 128)
        both = jnp.where(lane >= shift, sums[first], sums[first + 1])
        rows = pltpu.roll(both, lax.rem(128 - shift, 128), 1)
        rows = fanned(jnp.where(lane < count, rows, 0.0), 32)
        rows = rows + pltpu.roll(rows, 6, 0)
        rows = rows + pltpu.roll(rows, 7, 0)
        at = k // (Z * Y_LOW) * Z + k % Z
        partial[at, k // Z % Y_LOW, 0:1, :] = rows[0:1, :]
        partial[at, k // Z % Y_LOW, 1:2, :] = rows[4:5, :]

    recv[place] = partial[place]
    pl.semaphore_wait(barrier, PLANE + Y_LOW * REPS - 2)

    def send(offset):
        peer = plane_peer(offset)
        pltpu.make_async_remote_copy(
            src_ref=partial.at[peer],
            dst_ref=recv.at[place],
            send_sem=send_sem,
            recv_sem=recv_sem,
            device_id={"blk": team_of(peer, low), "rep": rep},
            device_id_type=MESH,
        ).start()

    for_peers(PLANE, 23, send)
    pltpu.make_async_copy(recv.at[pl.ds(0, PLANE - 1)], recv.at[pl.ds(0, PLANE - 1)], recv_sem).wait()
    summed = jnp.sum(recv[...], axis=0)
    mine[...] = summed
    column[low, phase_of(team, rep)] = mine[low]

    def pass_on(step, carry):
        peer_low, peer_rep = column_peer(step)
        peer = team_of(place, peer_low)
        pltpu.make_async_remote_copy(
            src_ref=mine.at[peer_low],
            dst_ref=column.at[low, phase_of(peer, rep)],
            send_sem=send_sem2,
            recv_sem=recv_sem2,
            device_id={"blk": peer, "rep": peer_rep},
            device_id_type=MESH,
        ).start()
        return carry

    lax.fori_loop(1, Y_LOW * REPS, pass_on, 0)
    pltpu.make_async_copy(recv.at[pl.ds(0, PLANE - 1)], recv.at[pl.ds(0, PLANE - 1)], send_sem).wait()
    flat = partial.at[pl.ds(0, Y_LOW * REPS - 1), 0]
    pltpu.make_async_copy(flat, flat, recv_sem2).wait()
    pltpu.make_async_copy(flat, flat, send_sem2).wait()
    ring_out[...] = column[0] + column[1]


def finish_kernel(ring, live, force, new_jerk):
    source = iota((CAP, CAP), 0)
    slot = iota((CAP, CAP), 1)
    place = jnp.where(slot == lax.rem(source, SHARE) * REPS + lax.div(source, SHARE), 1.0, 0.0).astype(BF16)
    lane = iota((8, 128), 1)
    sub = iota((8, 128), 0)
    halves = []
    for half in range(2):
        tile = jnp.zeros((8, 128), F32)
        for k in range(4):
            message = ring[half * 4 + k]
            rows = jnp.where(sub < 4, message[0:1, :], message[1:2, :])
            rows = fanned(rows, 96)
            rows = rows if k == 0 else pltpu.roll(rows, 32 * k, 1)
            tile = jnp.where(lane // 32 == k, rows, tile)
        halves.append(tile)
    x = jnp.concatenate(halves, 1)
    a, b, c = (part.astype(F32) for part in split3(x))
    stack = jnp.concatenate([a, b, c, jnp.zeros((8, CAP), F32)], 0).astype(BF16)
    moved = jnp.dot(stack, place, preferred_element_type=F32)
    sums = moved[0:8] + moved[8:16] + moved[16:24]
    scaled = jnp.where(live[...] >= 0, sums / (STARS_DEV * TEAMS), 0.0)
    force[...] = scaled[0:3]
    new_jerk[...] = scaled[3:6]


def in_vmem():
    return pl.BlockSpec(memory_space=pltpu.VMEM)


def in_smem():
    return pl.BlockSpec(memory_space=pltpu.SMEM)


def anywhere():
    return pl.BlockSpec(memory_space=pl.ANY)


def pairs(offset, targets, field, columns):
    return pl.pallas_call(
        pair_kernel,
        out_shape=(
            jax.ShapeDtypeStruct((MAX_ROWS // 128 + 2, 8, 128), F32),
            jax.ShapeDtypeStruct((8, 128), F32),
        ),
        in_specs=[anywhere()] * 4,
        out_specs=(in_vmem(),) * 2,
        scratch_shapes=[
            pltpu.SMEM((1, 128), jnp.int32),
            pltpu.VMEM((TEAMS, 2, 128), F32),
            pltpu.VMEM((8, STARS_DEV), F32),
            pltpu.VMEM((STARS_DEV, 128), BF16),
            pltpu.SemaphoreType.DMA((4,)),
            pltpu.VMEM((8, MAX_ROWS + 256), F32),
            pltpu.VMEM((6, MAX_ROWS, 128), F32),
            pltpu.VMEM((MAX_ROWS, 128), F32),
            pltpu.VMEM((MAX_ROWS, 128), F32),
        ],
        compiler_params=pltpu.CompilerParams(vmem_limit_bytes=56 * 2**20),
        name="pairs",
    )(offset, targets, field, columns)


def body(position, velocity, accel, jerk, mass, elapsed, active_index):
    shape = jax.ShapeDtypeStruct
    message = pltpu.VMEM((TEAMS, 2, 128), F32)
    row = pltpu.VMEM((1, STARS_DEV), F32)
    triple = pltpu.VMEM((3, STARS_DEV), F32)
    dma = pltpu.SemaphoreType.DMA
    targets, offset, field, columns = pl.pallas_call(
        share_kernel,
        out_shape=(
            shape((TEAMS, 2, 128), F32),
            shape((1, 128), jnp.int32),
            shape((8, STARS_DEV), F32),
            shape((STARS_DEV, 128), BF16),
        ),
        in_specs=[in_smem()] + [anywhere()] * 6,
        out_specs=(in_vmem(), in_vmem(), anywhere(), anywhere()),
        scratch_shapes=[triple] * 4
        + [row] * 2
        + [
            pltpu.VMEM((8, STARS_DEV), F32),
            pltpu.VMEM((STARS_DEV, 128), BF16),
            pltpu.VMEM((2, 128), F32),
            message,
            dma((6,)),
            dma((2,)),
            dma,
            dma,
        ],
        compiler_params=pltpu.CompilerParams(collective_id=0, has_side_effects=True, vmem_limit_bytes=56 * 2**20),
        name="share",
    )(active_index, position, velocity, accel, jerk, mass[None, :], elapsed[None, :])
    sums, first_rows = pairs(offset, targets, field, columns)
    ring = pl.pallas_call(
        total_kernel,
        out_shape=shape((REPS, 2, 128), F32),
        in_specs=[in_smem(), in_vmem()] + [anywhere()] * 3,
        out_specs=in_vmem(),
        scratch_shapes=[
            pltpu.VMEM((MAX_ROWS // 128 + 2, 8, 128), F32),
            pltpu.VMEM((8, STARS_DEV), F32),
            pltpu.VMEM((STARS_DEV, 128), BF16),
            pltpu.VMEM((6, 128, 128), F32),
            pltpu.VMEM((128, 128), F32),
            pltpu.VMEM((128, 128), F32),
            pltpu.VMEM((PLANE, Y_LOW, 2, 128), F32),
            pltpu.VMEM((PLANE, Y_LOW, 2, 128), F32),
            pltpu.VMEM((Y_LOW, 2, 128), F32),
            pltpu.VMEM((Y_LOW, REPS, 2, 128), F32),
            dma((6,)),
        ]
        + [dma] * 4,
        compiler_params=pltpu.CompilerParams(collective_id=1, has_side_effects=True, vmem_limit_bytes=56 * 2**20),
        name="totals",
    )(offset, first_rows, sums, field, columns)
    return pl.pallas_call(
        finish_kernel,
        out_shape=(shape((3, CAP), F32), shape((3, CAP), F32)),
        in_specs=[in_vmem(), in_vmem()],
        out_specs=(in_vmem(),) * 2,
        name="finish",
    )(ring, active_index[None, :])


def solution(mesh):
    in_specs = (
        P(None, "blk"),
        P(None, "blk"),
        P(None, "blk"),
        P(None, "blk"),
        P("blk"),
        P("blk"),
        P("blk"),
    )
    out_specs = (P(None, "blk"), P(None, "blk"))
    return jax.shard_map(body, mesh=mesh, in_specs=in_specs, out_specs=out_specs, check_vma=False)
```

```python
import functools

import jax
import jax.numpy as jnp
from jax import lax
from jax.experimental import pallas as pl
from jax.experimental.pallas import tpu as pltpu
from jax.sharding import PartitionSpec as P

SOFTENING = 0.001
MESH = pl.DeviceIdType.MESH
F32 = jnp.float32
BF16 = jnp.bfloat16
TEAMS = 64
REPS = 8
CAP = 256
SHARE = CAP // REPS
Z = 8
Y_LOW = 2
PLANE = TEAMS // Y_LOW
STARS_DEV = 8192
MAX_ROWS = TEAMS * SHARE
GROUP = 16
EARLY = 128
UNROLL = 32


def iota(shape, dim):
    return lax.broadcasted_iota(jnp.int32, shape, dim)


def phase_of(team, rep):
    return lax.rem(rep + 3 * team, REPS)


def split3(x):
    a = x.astype(BF16)
    rest = x - a.astype(F32)
    b = rest.astype(BF16)
    c = (rest - b.astype(F32)).astype(BF16)
    return a, b, c


def fanned(rows, unit):
    sub = lax.rem(iota((8, 128), 0), 4)
    out = rows
    for k in range(1, 4):
        out = jnp.where(sub == k, pltpu.roll(rows, unit * k % 128, 1), out)
    return out


def for_peers(size, far, act):
    def down(k, carry):
        act(far - k)
        return carry

    def rest(k, carry):
        act(size - 1 - k)
        return carry

    lax.fori_loop(0, far, down, 0)
    lax.fori_loop(0, size - 1 - far, rest, 0)


def copy_all(pairs, sems):
    copies = [pltpu.make_async_copy(src, dst, sems.at[k]) for k, (src, dst) in enumerate(pairs)]
    for copy in copies:
        copy.start()
    return copies


def share_kernel(
    index_ref,
    pos_hbm,
    vel_hbm,
    acc_hbm,
    jrk_hbm,
    mass_hbm,
    elapsed_hbm,
    targets_out,
    offset_out,
    field_hbm,
    columns_hbm,
    pos,
    vel,
    acc,
    jrk,
    mass,
    elapsed,
    field,
    columns,
    own,
    recv,
    load_sem,
    store_sem,
    send_sem,
    recv_sem,
):
    team = lax.axis_index("blk")
    rep = lax.axis_index("rep")
    barrier = pltpu.get_barrier_semaphore()
    loads = copy_all(
        [(pos_hbm, pos), (vel_hbm, vel), (acc_hbm, acc), (jrk_hbm, jrk), (mass_hbm, mass), (elapsed_hbm, elapsed)],
        load_sem,
    )

    def greet(offset):
        peer = lax.rem(team + offset, TEAMS)
        pl.semaphore_signal(barrier, inc=1, device_id={"blk": peer}, device_id_type=MESH)

    for_peers(TEAMS, 47, greet)
    for copy in loads:
        copy.wait()

    h = elapsed[...]
    v, a, j = vel[...], acc[...], jrk[...]
    field[0:3, :] = pos[...] + h * (v + h * (0.5 * a + h / 6.0 * j))
    field[3:6, :] = v + h * (a + 0.5 * h * j)
    field[6:7, :] = mass[...]
    field[7:8, :] = jnp.ones((1, STARS_DEV), F32)
    stores = [pltpu.make_async_copy(field, field_hbm, store_sem.at[0])]
    stores[0].start()

    phase = phase_of(team, rep)
    lane = iota((8, 128), 1)
    sub = iota((8, 128), 0)
    picked = jnp.zeros((8, 128), F32)
    for group in range(2):
        slots = range(group * 16, group * 16 + 16)
        local = [index_ref[REPS * k + phase] - team * STARS_DEV for k in slots]

        def look(step, found):
            for k in range(4):
                at = pl.multiple_of(step * 512 + k * 128, 128)
                tile = field[:, pl.ds(at, 128)]
                number = lane + at
                found = tuple(jnp.where(number == want, tile, old) for want, old in zip(local, found))
            return found

        found = lax.fori_loop(0, STARS_DEV // 512, look, (jnp.zeros((8, 128), F32),) * 16)
        for k, one in zip(slots, found):
            picked = jnp.where(lane == k, jnp.sum(one, axis=1, keepdims=True), picked)
    picked = jnp.where(sub == 6, pltpu.roll(picked, 7, 0), picked)
    spread = fanned(jnp.where(lane < SHARE, picked, 0.0), 32)
    spread = spread + pltpu.roll(spread, 6, 0)
    spread = spread + pltpu.roll(spread, 7, 0)
    own[0:1, :] = spread[0:1, :]
    own[1:2, :] = spread[4:5, :]
    recv[team] = jnp.concatenate([spread[0:1, :], spread[4:5, :]], 0)

    pl.semaphore_wait(barrier, TEAMS - 1)

    def send(offset):
        pltpu.make_async_remote_copy(
            src_ref=own,
            dst_ref=recv.at[team],
            send_sem=send_sem,
            recv_sem=recv_sem,
            device_id={"blk": lax.rem(team + offset, TEAMS)},
            device_id_type=MESH,
        ).start()

    for_peers(TEAMS, 47, send)

    def source_tile(step, carry):
        for k in range(4):
            at = pl.multiple_of(step * 512 + k * 128, 128)
            rows = field[:, pl.ds(at, 128)]
            weighted = jnp.where(sub < 6, rows * rows[6:7, :], rows)
            a, b, c = (part.astype(F32) for part in split3(weighted))
            stack = jnp.concatenate([a, b, c, jnp.zeros((104, 128), F32)], 0)
            columns[pl.ds(at, 128), :] = jnp.transpose(stack).astype(BF16)
        return carry

    lax.fori_loop(0, STARS_DEV // 512, source_tile, 0)
    stores.append(pltpu.make_async_copy(columns, columns_hbm, store_sem.at[1]))
    stores[1].start()
    pltpu.make_async_copy(recv.at[pl.ds(0, TEAMS - 1)], recv.at[pl.ds(0, TEAMS - 1)], recv_sem).wait()
    pltpu.make_async_copy(recv.at[pl.ds(0, TEAMS - 1)], recv.at[pl.ds(0, TEAMS - 1)], send_sem).wait()
    got = recv[...]
    targets_out[...] = got
    flag_lanes = iota((TEAMS, 128), 1)
    flags = jnp.where((flag_lanes >= 64) & (flag_lanes < 96), got[:, 1, :], 0.0)
    counts = jnp.sum(flags, axis=1, keepdims=True)
    before = jnp.where(iota((TEAMS, 128), 0) < flag_lanes, counts, 0.0)
    offset_out[...] = jnp.sum(before, axis=0, keepdims=True).astype(jnp.int32)
    for copy in stores:
        copy.wait()


def spread_targets(rows, tb, at):
    for k in range(6):
        tb[k, pl.ds(at, 128), :] = jnp.transpose(jnp.broadcast_to(rows[k : k + 1, :], (128, 128)))


def folded_sums(rows, sum_s, sum_t, at):
    sub = iota((8, 128), 0)

    def folded(ref):
        cols = jnp.transpose(ref[pl.ds(at, 128), :])
        part = cols[0:8] + cols[8:16] + cols[16:24]
        return part - rows * part[6:7, :]

    g_s, g_t = folded(sum_s), folded(sum_t)
    g_t = pltpu.roll(g_t, 3, 0)
    out = jnp.where((sub >= 3) & (sub < 6), g_s - 3.0 * g_t, g_s)
    return jnp.where(sub < 6, out, 0.0)


def block_adder(field, columns, tb, sum_s, sum_t):
    chunks = STARS_DEV // 512

    def stage(chunk, register):
        for m in range(2):
            cols = pl.ds(pl.multiple_of(chunk * 512 + m * 256, 256), 256)
            rhs = jnp.concatenate([columns[cols, :], jnp.zeros((256, 128), BF16)], 1)
            pltpu.matmul_push_rhs(rhs, register, m)

    def add_chunk(at, chunk, register, acc_s, acc_t):
        for g in range(len(acc_s[0])):
            rows = pl.ds(at + g * GROUP, GROUP)
            for m in range(2):
                parts = [[], [], [], []]
                for half in range(2):
                    cols = pl.ds(pl.multiple_of(chunk * 512 + m * 256 + half * 128, 128), 128)
                    d = [field[c : c + 1, cols] - tb[c, rows, :] for c in range(3)]
                    w = [field[c + 3 : c + 4, cols] - tb[c + 3, rows, :] for c in range(3)]
                    r2 = d[0] * d[0] + d[1] * d[1] + d[2] * d[2] + SOFTENING
                    q = lax.rsqrt(r2)
                    u = d[0] * w[0] + d[1] * w[1] + d[2] * w[2]
                    q2 = q * q
                    s = q * q2
                    t = (u * q2) * s
                    s_hi, t_hi = s.astype(BF16), t.astype(BF16)
                    parts[0].append(s_hi)
                    parts[1].append(s - s_hi.astype(F32))
                    parts[2].append(t_hi)
                    parts[3].append(t - t_hi.astype(F32))
                parts = [jnp.concatenate(pair, 1) for pair in parts]
                first = register if g == 0 else None
                pltpu.matmul_acc_lhs(acc_s[m][g], parts[0], load_staged_rhs=first)
                pltpu.matmul_acc_lhs(acc_s[m][g], parts[1])
                pltpu.matmul_acc_lhs(acc_t[m][g], parts[2])
                pltpu.matmul_acc_lhs(acc_t[m][g], parts[3])

    def add_blocks(size, base, count, unroll, before=None):
        groups = size // GROUP

        def scoped(*accs):
            acc_s = [accs[m * groups : (m + 1) * groups] for m in range(2)]
            acc_t = [accs[(2 + m) * groups : (3 + m) * groups] for m in range(2)]

            def block(number, carry):
                at = pl.multiple_of(base + number * size, 32)
                stage(0, 0)

                def some_chunks(step, inner):
                    if before is not None:
                        before(step)
                    for k in range(unroll):
                        chunk = step * unroll + k
                        stage(jnp.minimum(chunk + 1, chunks - 1), 1 - k % 2)
                        add_chunk(at, chunk, k % 2, acc_s, acc_t)
                    return inner

                lax.fori_loop(0, chunks // unroll, some_chunks, 0)
                for g in range(groups):
                    rows = pl.ds(at + g * GROUP, GROUP)
                    sum_s[rows, :] = pltpu.matmul_pop(acc_s[0][g])[:, :128] + pltpu.matmul_pop(acc_s[1][g])[:, :128]
                    sum_t[rows, :] = pltpu.matmul_pop(acc_t[0][g])[:, :128] + pltpu.matmul_pop(acc_t[1][g])[:, :128]
                for m in range(2):
                    pltpu.matmul_acc_lhs(acc_s[m][0], jnp.zeros((GROUP, 256), BF16), load_staged_rhs=0)
                    pltpu.matmul_pop(acc_s[m][0])
                return carry

            lax.fori_loop(0, count, block, 0)

        sets = []
        for m in (0, 1, 0, 1):
            sets += [pltpu.ACC(m)((GROUP, 256), F32)] * groups
        pl.run_scoped(scoped, *sets)

    return add_blocks


def pair_kernel(
    offset_hbm, targets_hbm, field_hbm, columns_hbm, sums_out, first_out,
    offset, targets, field, columns, load_sem, comp, tb, sum_s, sum_t,
):
    loads = copy_all(
        [(offset_hbm, offset), (targets_hbm, targets), (field_hbm, field), (columns_hbm, columns)], load_sem
    )
    lane = iota((8, 128), 1)
    sub = iota((8, 128), 0)
    loads[0].wait()
    loads[1].wait()
    total = offset[0, TEAMS]
    tiles = lax.div(total + 127, 128)

    def clear(tile, carry):
        comp[:, pl.ds(pl.multiple_of(tile * 128, 128), 128)] = jnp.zeros((8, 128), F32)
        return carry

    lax.fori_loop(0, tiles + 2, clear, 0)

    def compact(step, carry):
        ready = []
        for k in range(UNROLL):
            team = step * UNROLL + k
            start = offset[0, team]
            count = offset[0, team + 1] - start
            message = targets[team]
            rows = jnp.where(sub < 4, message[0:1, :], message[1:2, :])
            rows = jnp.where(lane < count, fanned(rows, 96), 0.0)
            shift = lax.rem(start, 128)
            ready.append((pl.multiple_of(lax.div(start, 128) * 128, 128), shift, pltpu.roll(rows, shift, 1)))
        for first, shift, rows in ready:
            comp[:, pl.ds(first, 128)] += jnp.where(lane >= shift, rows, 0.0)
            comp[:, pl.ds(first + 128, 128)] += jnp.where(lane < shift, rows, 0.0)
        return carry

    lax.fori_loop(0, TEAMS // UNROLL, compact, 0)

    def target_tile(tile, carry):
        at = pl.multiple_of(tile * 128, 128)
        spread_targets(comp[:, pl.ds(at, 128)], tb, at)
        return carry

    lax.fori_loop(0, tiles, target_tile, 0)
    first_out[...] = comp[:, 0:128]
    loads[2].wait()
    loads[3].wait()

    add_blocks = block_adder(field, columns, tb, sum_s, sum_t)
    left = jnp.maximum(total - EARLY, 0)
    whole = lax.div(left, 96)
    rest = left - whole * 96
    base = EARLY + whole * 96
    one = jnp.int32(1)
    none = jnp.int32(0)
    add_blocks(96, EARLY, whole + jnp.where(rest > 64, one, none), 4)
    add_blocks(64, base, jnp.where((rest > 32) & (rest <= 64), one, none), 4)
    add_blocks(32, base, jnp.where((rest > 0) & (rest <= 32), one, none), 4)

    def result_tile(tile, carry):
        at = pl.multiple_of(tile * 128, 128)
        sums_out[tile] = folded_sums(comp[:, pl.ds(at, 128)], sum_s, sum_t, at)
        return carry

    lax.fori_loop(0, tiles, result_tile, 0)


def total_kernel(
    offset, first_rows, sums_hbm, field_hbm, columns_hbm, ring_out,
    sums, field, columns, tb, sum_s, sum_t, partial, recv, mine, column,
    load_sem, send_sem, recv_sem, send_sem2, recv_sem2,
):
    team = lax.axis_index("blk")
    rep = lax.axis_index("rep")
    depth = lax.rem(team, Z)
    low = lax.rem(lax.div(team, Z), Y_LOW)
    wide = lax.div(team, Z * Y_LOW)
    place = wide * Z + depth
    stack = low * REPS + rep

    def team_of(place, low):
        return (lax.div(place, Z) * Y_LOW + low) * Z + lax.rem(place, Z)

    def plane_peer(step):
        return lax.rem(place + step, PLANE)

    def column_peer(step):
        other = lax.rem(stack + step, Y_LOW * REPS)
        return lax.div(other, REPS), lax.rem(other, REPS)

    barrier = pltpu.get_barrier_semaphore()

    def quarter(n):
        return columns_hbm.at[pl.ds(n * 2048, 2048)], columns.at[pl.ds(n * 2048, 2048)]

    loads = copy_all([(field_hbm, field)] + [quarter(n) for n in range(4)] + [(sums_hbm, sums)], load_sem)

    def greet_plane(offset):
        peer = team_of(plane_peer(offset), low)
        pl.semaphore_signal(barrier, inc=1, device_id={"blk": peer, "rep": rep}, device_id_type=MESH)

    def greet_column(step, carry):
        peer_low, peer_rep = column_peer(step)
        pl.semaphore_signal(
            barrier, inc=1, device_id={"blk": team_of(place, peer_low), "rep": peer_rep}, device_id_type=MESH
        )
        return carry

    for_peers(PLANE, 23, greet_plane)
    lax.fori_loop(1, Y_LOW * REPS, greet_column, 0)

    spread_targets(first_rows[...], tb, 0)
    loads[0].wait()
    loads[1].wait()

    def await_quarter(step):
        @pl.when(step < 3)
        def _():
            ahead = pl.multiple_of(step * 2048 + 2048, 2048)
            pltpu.make_async_copy(
                columns_hbm.at[pl.ds(ahead, 2048)], columns.at[pl.ds(ahead, 2048)], load_sem.at[step + 2]
            ).wait()

    block_adder(field, columns, tb, sum_s, sum_t)(EARLY, 0, 1, 4, await_quarter)
    loads[5].wait()
    lane = iota((8, 128), 1)
    sums[0] = jnp.where(lane < EARLY, folded_sums(first_rows[...], sum_s, sum_t, 0), sums[0])

    for k in range(TEAMS):
        start = offset[0, k]
        count = offset[0, k + 1] - start
        first = lax.div(start, 128)
        shift = lax.rem(start, 128)
        both = jnp.where(lane >= shift, sums[first], sums[first + 1])
        rows = pltpu.roll(both, lax.rem(128 - shift, 128), 1)
        rows = fanned(jnp.where(lane < count, rows, 0.0), 32)
        rows = rows + pltpu.roll(rows, 6, 0)
        rows = rows + pltpu.roll(rows, 7, 0)
        at = k // (Z * Y_LOW) * Z + k % Z
        partial[at, k // Z % Y_LOW, 0:1, :] = rows[0:1, :]
        partial[at, k // Z % Y_LOW, 1:2, :] = rows[4:5, :]

    recv[place] = partial[place]
    pl.semaphore_wait(barrier, PLANE + Y_LOW * REPS - 2)

    def send(offset):
        peer = plane_peer(offset)
        pltpu.make_async_remote_copy(
            src_ref=partial.at[peer],
            dst_ref=recv.at[place],
            send_sem=send_sem,
            recv_sem=recv_sem,
            device_id={"blk": team_of(peer, low), "rep": rep},
            device_id_type=MESH,
        ).start()

    for_peers(PLANE, 23, send)
    pltpu.make_async_copy(recv.at[pl.ds(0, PLANE - 1)], recv.at[pl.ds(0, PLANE - 1)], recv_sem).wait()
    summed = jnp.sum(recv[...], axis=0)
    mine[...] = summed
    column[low, phase_of(team, rep)] = mine[low]

    def pass_on(step, carry):
        peer_low, peer_rep = column_peer(step)
        peer = team_of(place, peer_low)
        pltpu.make_async_remote_copy(
            src_ref=mine.at[peer_low],
            dst_ref=column.at[low, phase_of(peer, rep)],
            send_sem=send_sem2,
            recv_sem=recv_sem2,
            device_id={"blk": peer, "rep": peer_rep},
            device_id_type=MESH,
        ).start()
        return carry

    lax.fori_loop(1, Y_LOW * REPS, pass_on, 0)
    pltpu.make_async_copy(recv.at[pl.ds(0, PLANE - 1)], recv.at[pl.ds(0, PLANE - 1)], send_sem).wait()
    flat = partial.at[pl.ds(0, Y_LOW * REPS - 1), 0]
    pltpu.make_async_copy(flat, flat, recv_sem2).wait()
    pltpu.make_async_copy(flat, flat, send_sem2).wait()
    ring_out[...] = column[0] + column[1]


def finish_kernel(ring_hbm, live_hbm, force, new_jerk, ring, live, load_sem):
    loads = copy_all([(ring_hbm, ring), (live_hbm, live)], load_sem)
    source = iota((CAP, CAP), 0)
    slot = iota((CAP, CAP), 1)
    place = jnp.where(slot == lax.rem(source, SHARE) * REPS + lax.div(source, SHARE), 1.0, 0.0).astype(BF16)
    for copy in loads:
        copy.wait()
    lane = iota((8, 128), 1)
    sub = iota((8, 128), 0)
    halves = []
    for half in range(2):
        tile = jnp.zeros((8, 128), F32)
        for k in range(4):
            message = ring[half * 4 + k]
            rows = jnp.where(sub < 4, message[0:1, :], message[1:2, :])
            rows = fanned(rows, 96)
            rows = rows if k == 0 else pltpu.roll(rows, 32 * k, 1)
            tile = jnp.where(lane // 32 == k, rows, tile)
        halves.append(tile)
    x = jnp.concatenate(halves, 1)
    a, b, c = (part.astype(F32) for part in split3(x))
    stack = jnp.concatenate([a, b, c, jnp.zeros((8, CAP), F32)], 0).astype(BF16)
    moved = jnp.dot(stack, place, preferred_element_type=F32)
    sums = moved[0:8] + moved[8:16] + moved[16:24]
    scaled = jnp.where(live[...] >= 0, sums / (STARS_DEV * TEAMS), 0.0)
    force[...] = scaled[0:3]
    new_jerk[...] = scaled[3:6]


def in_vmem():
    return pl.BlockSpec(memory_space=pltpu.VMEM)


def in_smem():
    return pl.BlockSpec(memory_space=pltpu.SMEM)


def anywhere():
    return pl.BlockSpec(memory_space=pl.ANY)


def pairs(offset, targets, field, columns):
    return pl.pallas_call(
        pair_kernel,
        out_shape=(
            jax.ShapeDtypeStruct((MAX_ROWS // 128 + 2, 8, 128), F32),
            jax.ShapeDtypeStruct((8, 128), F32),
        ),
        in_specs=[anywhere()] * 4,
        out_specs=(in_vmem(),) * 2,
        scratch_shapes=[
            pltpu.SMEM((1, 128), jnp.int32),
            pltpu.VMEM((TEAMS, 2, 128), F32),
            pltpu.VMEM((8, STARS_DEV), F32),
            pltpu.VMEM((STARS_DEV, 128), BF16),
            pltpu.SemaphoreType.DMA((4,)),
            pltpu.VMEM((8, MAX_ROWS + 256), F32),
            pltpu.VMEM((6, MAX_ROWS, 128), F32),
            pltpu.VMEM((MAX_ROWS, 128), F32),
            pltpu.VMEM((MAX_ROWS, 128), F32),
        ],
        compiler_params=pltpu.CompilerParams(vmem_limit_bytes=56 * 2**20),
        name="pairs",
    )(offset, targets, field, columns)


def body(position, velocity, accel, jerk, mass, elapsed, active_index):
    shape = jax.ShapeDtypeStruct
    message = pltpu.VMEM((TEAMS, 2, 128), F32)
    row = pltpu.VMEM((1, STARS_DEV), F32)
    triple = pltpu.VMEM((3, STARS_DEV), F32)
    dma = pltpu.SemaphoreType.DMA
    targets, offset, field, columns = pl.pallas_call(
        share_kernel,
        out_shape=(
            shape((TEAMS, 2, 128), F32),
            shape((1, 128), jnp.int32),
            shape((8, STARS_DEV), F32),
            shape((STARS_DEV, 128), BF16),
        ),
        in_specs=[in_smem()] + [anywhere()] * 6,
        out_specs=(in_vmem(), in_vmem(), anywhere(), anywhere()),
        scratch_shapes=[triple] * 4
        + [row] * 2
        + [
            pltpu.VMEM((8, STARS_DEV), F32),
            pltpu.VMEM((STARS_DEV, 128), BF16),
            pltpu.VMEM((2, 128), F32),
            message,
            dma((6,)),
            dma((2,)),
            dma,
            dma,
        ],
        compiler_params=pltpu.CompilerParams(collective_id=0, has_side_effects=True, vmem_limit_bytes=56 * 2**20),
        name="share",
    )(active_index, position, velocity, accel, jerk, mass[None, :], elapsed[None, :])
    sums, first_rows = pairs(offset, targets, field, columns)
    ring = pl.pallas_call(
        total_kernel,
        out_shape=shape((REPS, 2, 128), F32),
        in_specs=[in_smem(), in_vmem()] + [anywhere()] * 3,
        out_specs=in_vmem(),
        scratch_shapes=[
            pltpu.VMEM((MAX_ROWS // 128 + 2, 8, 128), F32),
            pltpu.VMEM((8, STARS_DEV), F32),
            pltpu.VMEM((STARS_DEV, 128), BF16),
            pltpu.VMEM((6, 128, 128), F32),
            pltpu.VMEM((128, 128), F32),
            pltpu.VMEM((128, 128), F32),
            pltpu.VMEM((PLANE, Y_LOW, 2, 128), F32),
            pltpu.VMEM((PLANE, Y_LOW, 2, 128), F32),
            pltpu.VMEM((Y_LOW, 2, 128), F32),
            pltpu.VMEM((Y_LOW, REPS, 2, 128), F32),
            dma((6,)),
        ]
        + [dma] * 4,
        compiler_params=pltpu.CompilerParams(collective_id=1, has_side_effects=True, vmem_limit_bytes=56 * 2**20),
        name="totals",
    )(offset, first_rows, sums, field, columns)
    return pl.pallas_call(
        finish_kernel,
        out_shape=(shape((3, CAP), F32), shape((3, CAP), F32)),
        in_specs=[anywhere()] * 2,
        out_specs=(in_vmem(),) * 2,
        scratch_shapes=[
            pltpu.VMEM((REPS, 2, 128), F32),
            pltpu.VMEM((1, CAP), jnp.int32),
            pltpu.SemaphoreType.DMA((2,)),
        ],
        name="finish",
    )(ring, active_index[None, :])


def solution(mesh):
    in_specs = (
        P(None, "blk"),
        P(None, "blk"),
        P(None, "blk"),
        P(None, "blk"),
        P("blk"),
        P("blk"),
        P("blk"),
    )
    out_specs = (P(None, "blk"), P(None, "blk"))
    return jax.shard_map(body, mesh=mesh, in_specs=in_specs, out_specs=out_specs, check_vma=False)
```
